32 devices in a mesh: tm: 2 (over x), row: 4 (over z), col: 4 (over y, core).
Axes of the slice: x: 2, y: 2, z: 4, core: 2. Of those that a mesh axis runs over, the one named last changes fastest.
Arguments:
- occ_orbitals: bfloat16 [1024, 2048], P(('col', 'row'), 'tm'), may hold values from -0.4375 to 0.4375
- empty_orbitals: bfloat16 [1024, 2048], P(('col', 'row'), 'tm'), may hold values from -0.4375 to 0.4375
- occ_rate: float32 [2048], replicated, may hold values from 0.05 to 4
- empty_rate: float32 [2048], replicated, may hold values from 0.05 to 4
- columns: bfloat16 [1024, 256], P(('col', 'row')), may hold values from -6 to 6
Outputs:
- screened_columns: float32 [1024, 16, 256], P(('col', 'row'), 'tm')
The draws below stay inside these ranges and needn't reach their ends.
All inputs are finite; a program needn't handle non-finite values.
Results may differ from the reference program's by a relative error of at most 0.018.
Values may be sent and summed in bfloat16 or wider, within the bound.
No kernel may reach another device: no remote copies, remote signals or barrier semaphores. Data moves between devices by JAX's collectives and lax.ppermute only.
A program may use at most 64 MiB of HBM per device.

```python
import math
import jax
import jax.numpy as jnp
from jax import lax

NO = 2048
NE = 2048
NT = 16
NF = 16
NC = 256
ROWS_DEV = 64
R = 1024
N_ROW = 4
N_COL = 4


def block_levels(key, shape, split, low, high):
    gain = 1.0
    for dim, shards_of in split:
        draws = jax.random.uniform(jax.random.fold_in(jax.random.fold_in(key, 6), dim), (shards_of,), jnp.float32, low / len(split), high / len(split))
        gain = gain * jnp.repeat(jnp.exp(draws), shape[dim] // shards_of).reshape((-1,) + (1,) * (len(shape) - 1 - dim))
    return gain


def scatter_about(rng, extent, scale, bound, cuts=(), kind=jnp.bfloat16):
    entries = scale * jax.random.normal(rng, extent, jnp.float32)
    if cuts:
        entries = entries * block_levels(rng, extent, cuts, -0.22, 0.18)
    return jnp.clip(entries, -bound, bound).astype(kind)


def setup_inputs(seed: int = 0) -> dict:
    arg_keys = jax.random.split(jax.random.key(seed), 6)
    return {
        "occ_orbitals": scatter_about(arg_keys[0], (R, NO), ((0.3 * NO * (NO + R ** 0.5)) ** -0.25), 0.4375, ((0, 16), (1, 2))),
        "empty_orbitals": scatter_about(arg_keys[1], (R, NE), ((0.3 * NE * (NE + R ** 0.5)) ** -0.25), 0.4375, ((0, 16), (1, 2))),
        "occ_rate": jnp.clip(jnp.exp(jax.random.uniform(arg_keys[2], (NO,), jnp.float32, math.log(0.05), math.log(4.0))), 0.05, 4.0),
        "empty_rate": jnp.clip(jnp.exp(jax.random.uniform(arg_keys[3], (NE,), jnp.float32, math.log(0.05), math.log(4.0))), 0.05, 4.0),
        "columns": scatter_about(arg_keys[4], (R, NC), 1.0, 6.0, ((0, 16),)),
    }


damping = 0.3


def time_tables(count_times, count_freqs):
    moments = 0.25 * (jnp.arange(count_times).astype(jnp.float32) + 0.5)
    omegas = 0.4 * (jnp.arange(count_freqs).astype(jnp.float32) + 0.5)
    cosine = (0.5 * jnp.cos(omegas[:, None] * moments[None, :])).astype(jnp.bfloat16)
    return moments, cosine


def spectral_block(occ_rows, empty_rows, occ_orbitals, empty_orbitals, occ_rate, empty_rate, moments, cosine):
    occ_full = occ_orbitals.astype(jnp.float32)
    empty_full = empty_orbitals.astype(jnp.float32)

    def one_time(moment):
        scaled_occ = (occ_rows.astype(jnp.float32) * jnp.exp(-occ_rate * moment)[None, :]).astype(jnp.bfloat16)
        scaled_empty = (empty_rows.astype(jnp.float32) * jnp.exp(-empty_rate * moment)[None, :]).astype(jnp.bfloat16)
        green_occ = jnp.einsum("ro,co->rc", scaled_occ.astype(jnp.float32), occ_full, precision=lax.Precision.HIGHEST)
        green_empty = jnp.einsum("ro,co->rc", scaled_empty.astype(jnp.float32), empty_full, precision=lax.Precision.HIGHEST)
        return (-2.0 * green_occ * green_empty).astype(jnp.bfloat16)

    polar = lax.map(one_time, moments)
    spectral = jnp.einsum("kj,jrc->krc", cosine.astype(jnp.float32), polar.astype(jnp.float32), precision=lax.Precision.HIGHEST)
    return spectral.astype(jnp.bfloat16)


def reference(occ_orbitals, empty_orbitals, occ_rate, empty_rate, columns):
    moments, cosine = time_tables(NT, NF)
    rows_tile = R // N_ROW
    block_count = N_ROW
    indices = jnp.arange(block_count).astype(jnp.int32)
    columns_wide = columns.astype(jnp.float32)

    def first_pass(index):
        start = (index * rows_tile).astype(jnp.int32)
        occ_rows = lax.dynamic_slice_in_dim(occ_orbitals, start, rows_tile, 0)
        empty_rows = lax.dynamic_slice_in_dim(empty_orbitals, start, rows_tile, 0)
        spectral = spectral_block(occ_rows, empty_rows, occ_orbitals, empty_orbitals, occ_rate, empty_rate, moments, cosine)
        return jnp.einsum("frc,cn->frn", spectral.astype(jnp.float32), columns_wide, precision=lax.Precision.HIGHEST)

    first = lax.map(first_pass, indices)
    first = jnp.transpose(first, (1, 0, 2, 3)).reshape(NF, R, NC)
    middle = (columns_wide[None, :, :] + damping * first).astype(jnp.bfloat16)
    group_span = ROWS_DEV * N_ROW
    base = (jnp.arange(N_COL).astype(jnp.int32)[:, None] * group_span + jnp.arange(ROWS_DEV).astype(jnp.int32)[None, :]).reshape(-1)

    def second_pass(total, index):
        picks = (base + index * ROWS_DEV).astype(jnp.int32)
        occ_rows = jnp.take(occ_orbitals, picks, axis=0)
        empty_rows = jnp.take(empty_orbitals, picks, axis=0)
        spectral = spectral_block(occ_rows, empty_rows, occ_orbitals, empty_orbitals, occ_rate, empty_rate, moments, cosine)
        middle_rows = jnp.take(middle, picks, axis=1)
        term = jnp.einsum("frc,frn->cfn", spectral.astype(jnp.float32), middle_rows.astype(jnp.float32), precision=lax.Precision.HIGHEST)
        rounded = lax.optimization_barrier(term.astype(jnp.bfloat16))
        return total + rounded.astype(jnp.float32), None

    second, unused = lax.scan(second_pass, jnp.zeros((R, NF, NC), jnp.float32), indices)
    return columns_wide[:, None, :] + damping * second
```

```python
import functools

import jax
import jax.numpy as jnp
from jax import lax
from jax.experimental import pallas as pl
from jax.experimental.pallas import tpu as pltpu
from jax.sharding import PartitionSpec as P

NT = 16
NF = 16

damping = 0.3

ANY = pl.BlockSpec(memory_space=pl.ANY)
VMEM = pl.BlockSpec(memory_space=pltpu.VMEM)
SMEM = pl.BlockSpec(memory_space=pltpu.SMEM)


def time_tables(count_times, count_freqs):
    moments = 0.25 * (jnp.arange(count_times).astype(jnp.float32) + 0.5)
    omegas = 0.4 * (jnp.arange(count_freqs).astype(jnp.float32) + 0.5)
    cosine = (0.5 * jnp.cos(omegas[:, None] * moments[None, :])).astype(jnp.bfloat16)
    return (moments, cosine)


def swap(value, axis, bit):
    size = lax.axis_size(axis)
    return lax.ppermute(value, axis, [(i, i ^ bit) for i in range(size)])


def shift(value, axis, step):
    size = lax.axis_size(axis)
    return lax.ppermute(value, axis, [(i, (i + step) % size) for i in range(size)])


def bits_of(count):
    return [1 << b for b in reversed(range(count.bit_length() - 1))]


def ring(value, axis):
    size = lax.axis_size(axis)
    blocks = {0: value}
    ahead = behind = value
    for k in range(1, size // 2 + 1):
        ahead = shift(ahead, axis, -1)
        blocks[k] = ahead
        if k <= (size - 1) // 2:
            behind = shift(behind, axis, 1)
            blocks[size - k] = behind
    return blocks


def spread(pieces, axis, bit, slot):
    out = dict(pieces)
    for key, value in pieces.items():
        moved = list(key)
        moved[slot] ^= bit
        out[tuple(moved)] = swap(value, axis, bit)
    return out


def tile_kernel(keys, dims, cosine, factors, *refs):
    (row_keys, col_keys) = keys
    (times, freqs, half, shard_rows, part, batch) = dims
    pieces = refs[: len(row_keys) + len(col_keys)]
    out, rows, cols, scaled, polar, sem = refs[len(pieces) :]
    tm, q, p = lax.axis_index("tm"), lax.axis_index("row"), lax.axis_index("col")
    row_count = rows.shape[1] // shard_rows
    col_count = cols.shape[1] // part
    copies = []
    for (arr, kt, kc), ref in zip(row_keys, pieces[: len(row_keys)]):
        to = pl.multiple_of((p ^ kc) * shard_rows, shard_rows)
        lane = pl.multiple_of((tm ^ kt) * half, half)
        copies.append((ref, rows.at[arr, pl.ds(to, shard_rows), pl.ds(lane, half)]))
    for (arr, kts, kq), ref in zip(col_keys, pieces[len(row_keys) :]):
        to = pl.multiple_of(lax.rem(q + kq, col_count) * part, part)
        for n, kt in enumerate(kts):
            lane = pl.multiple_of((tm ^ kt) * half, half)
            copies.append(
                (ref.at[:, pl.ds(n * half, half)], cols.at[arr, pl.ds(to, part), pl.ds(lane, half)])
            )
    copies = [pltpu.make_async_copy(a, b, sem) for a, b in copies]
    for copy in copies:
        copy.start()
    for copy in copies:
        copy.wait()
    width = cols.shape[1]

    def some_times(step, carry):
        greens = []
        for arr in range(2):
            for b in range(batch):
                factor = factors[arr, pl.ds(step * batch + b, 1), :]
                scaled[arr, pl.ds(b * width, width), :] = (
                    cols[arr].astype(jnp.float32) * factor
                ).astype(jnp.bfloat16)
            greens.append(
                lax.dot_general(
                    scaled[arr],
                    rows[arr],
                    (((1,), (1,)), ((), ())),
                    preferred_element_type=jnp.float32,
                )
            )
        product = (-2.0 * greens[0] * greens[1]).astype(jnp.bfloat16)
        polar[pl.ds(step * batch, batch)] = product.reshape(batch, width, rows.shape[1])
        return carry

    lax.fori_loop(0, times // batch, some_times, 0)
    chunk = 16
    lanes = 128

    def transform(index, carry):
        start = pl.multiple_of(index * chunk, chunk)
        for lane in range(0, rows.shape[1], lanes):
            values = [
                polar[j, pl.ds(start, chunk), pl.ds(lane, lanes)].astype(jnp.float32)
                for j in range(times)
            ]
            for k in range(freqs):
                total = values[0] * cosine[k, 0]
                for j in range(1, times):
                    total = total + values[j] * cosine[k, j]
                out[k, pl.ds(start, chunk), pl.ds(lane, lanes)] = total.astype(jnp.bfloat16)
        return carry

    lax.fori_loop(0, width // chunk, transform, 0)


def columns_kernel(keys, dims, *refs):
    (tm_count, row_count, col_count, shard_rows, part) = dims
    pieces = refs[: len(keys)]
    out, own, gathered, own_rows, sem = refs[len(keys) :]
    q, p = lax.axis_index("row"), lax.axis_index("col")
    width = row_count * part
    copies = []
    for (kq, kc), ref in zip(keys, pieces):
        for t in range(tm_count):
            to = (t * col_count + (p ^ kc)) * width + lax.rem(q + kq, row_count) * part
            to = pl.multiple_of(to, part)
            copies.append((ref.at[pl.ds(t * part, part), :], gathered.at[pl.ds(to, part), :]))
        if kq == 0:
            to = pl.multiple_of((p ^ kc) * shard_rows, shard_rows)
            copies.append((ref, own_rows.at[pl.ds(to, shard_rows), :]))
    copies = [pltpu.make_async_copy(a, b, sem) for a, b in copies]
    for copy in copies:
        copy.start()
    for copy in copies:
        copy.wait()
    out[...] = gathered[...].astype(jnp.float32).T.astype(jnp.bfloat16)
    own[...] = own_rows[...].astype(jnp.float32).T.astype(jnp.bfloat16)


def first_kernel(all_columns, own, tiles, out):
    sources, freqs, width, rows = tiles.shape
    for k in range(freqs):
        weights = tiles[:, k].reshape(sources * width, rows)
        first = jnp.dot(all_columns[...], weights, preferred_element_type=jnp.float32)
        out[k] = (own[...].astype(jnp.float32) + damping * first).astype(jnp.bfloat16)


def second_kernel(dims, tiles, *refs):
    (tm_count, row_count, col_count, part, shard_rows) = dims
    middles = refs[:row_count]
    out = refs[row_count]
    sources, freqs, width, rows = tiles.shape
    q = lax.axis_index("row")
    for k in range(freqs):
        total = None
        for kq in range(row_count):
            start = pl.multiple_of(lax.rem(q + kq, row_count) * part, part)
            weights = jnp.concatenate(
                [
                    tiles[t * col_count + p, k, pl.ds(start, part), :]
                    for p in range(col_count)
                    for t in range(tm_count)
                ],
                axis=0,
            )
            term = jnp.dot(middles[kq][k], weights, preferred_element_type=jnp.float32)
            total = term if total is None else total + term
        second = total.T.astype(jnp.bfloat16)
        for p in range(col_count):
            out[p, k] = second[p * shard_rows : (p + 1) * shard_rows]


def shards(occ_orbitals, empty_orbitals, occ_rate, empty_rate, columns):
    tm_count, row_count, col_count = (lax.axis_size(a) for a in ("tm", "row", "col"))
    shard_rows, half = occ_orbitals.shape
    columns_wide = columns.shape[1]
    orbitals = tm_count * half
    part = shard_rows // tm_count
    width = row_count * part
    tile_rows = col_count * shard_rows
    tm_index, col_index = lax.axis_index("tm"), lax.axis_index("col")
    both = (occ_orbitals, empty_orbitals)
    high, low = bits_of(col_count)[:-1], bits_of(col_count)[-1:]

    col_pieces = {}
    for arr, value in enumerate(both):
        held = []
        for kt in range(tm_count):
            block = lax.dynamic_slice_in_dim(value, (tm_index ^ kt) * part, part, 0)
            held.append(swap(block, "tm", kt) if kt else block)
        groups = [((kt,), block) for kt, block in enumerate(held)]
        if tm_count > 2:
            groups = [(tuple(range(tm_count)), jnp.concatenate(held, axis=1))]
        for kts, block in groups:
            for kq, moved in ring(block, "row").items():
                col_pieces[(arr, kts, kq)] = moved
    row_pieces = {}
    for arr, value in enumerate(both):
        pieces = {(arr, 0, 0): value}
        steps = [("tm", b, 1) for b in bits_of(tm_count)], [("col", b, 2) for b in high]
        order = steps[1] + steps[0] if arr == 0 else steps[0] + steps[1]
        for axis, bit, slot in order + [("col", b, 2) for b in low]:
            pieces = spread(pieces, axis, bit, slot)
        row_pieces.update(pieces)
    column_pieces = {(kq, 0): moved for kq, moved in ring(columns, "row").items()}
    for bit in high + low:
        column_pieces = spread(column_pieces, "col", bit, 1)

    moments, cosine = time_tables(NT, NF)
    factors = jnp.exp(-jnp.stack([occ_rate, empty_rate])[:, None, :] * moments[None, :, None])
    row_keys, col_keys = list(row_pieces), list(col_pieces)
    batch = 4
    tile = pl.pallas_call(
        functools.partial(
            tile_kernel, (row_keys, col_keys), (NT, NF, half, shard_rows, part, batch)
        ),
        out_shape=jax.ShapeDtypeStruct((NF, width, tile_rows), jnp.bfloat16),
        in_specs=[SMEM, VMEM] + [ANY] * (len(row_keys) + len(col_keys)),
        out_specs=VMEM,
        scratch_shapes=[
            pltpu.VMEM((2, tile_rows, orbitals), jnp.bfloat16),
            pltpu.VMEM((2, width, orbitals), jnp.bfloat16),
            pltpu.VMEM((2, batch * width, orbitals), jnp.bfloat16),
            pltpu.VMEM((NT, width, tile_rows), jnp.bfloat16),
            pltpu.SemaphoreType.DMA,
        ],
        name="tile",
    )(
        cosine.astype(jnp.float32),
        factors,
        *[row_pieces[k] for k in row_keys],
        *[col_pieces[k] for k in col_keys],
    )

    keys = list(column_pieces)
    all_columns, own = pl.pallas_call(
        functools.partial(
            columns_kernel, keys, (tm_count, row_count, col_count, shard_rows, part)
        ),
        out_shape=(
            jax.ShapeDtypeStruct((columns_wide, tm_count * col_count * width), jnp.bfloat16),
            jax.ShapeDtypeStruct((columns_wide, tile_rows), jnp.bfloat16),
        ),
        in_specs=[ANY] * len(keys),
        out_specs=(VMEM, VMEM),
        scratch_shapes=[
            pltpu.VMEM((tm_count * col_count * width, columns_wide), jnp.bfloat16),
            pltpu.VMEM((tile_rows, columns_wide), jnp.bfloat16),
            pltpu.SemaphoreType.DMA,
        ],
        name="columns",
    )(*[column_pieces[k] for k in keys])

    local_freqs = NF // tm_count
    own_freqs = max(1, local_freqs // col_count)
    splits = max(1, col_count // local_freqs)
    columns_own = columns_wide // splits
    sent = tile.reshape(NF // own_freqs, own_freqs, width, tile_rows)
    if splits > 1:
        sent = jnp.repeat(sent, splits, axis=0)
        first_row = (col_index % splits) * columns_own
        all_columns = lax.dynamic_slice_in_dim(all_columns, first_row, columns_own, 0)
        own = lax.dynamic_slice_in_dim(own, first_row, columns_own, 0)
    tiles = lax.all_to_all(sent, ("tm", "col"), split_axis=0, concat_axis=0, tiled=True)

    middle = pl.pallas_call(
        first_kernel,
        out_shape=jax.ShapeDtypeStruct((own_freqs, columns_own, tile_rows), jnp.bfloat16),
        in_specs=[VMEM, VMEM, VMEM],
        out_specs=VMEM,
        name="first",
    )(all_columns, own, tiles)
    middles = ring(middle, "row")
    second = pl.pallas_call(
        functools.partial(second_kernel, (tm_count, row_count, col_count, part, shard_rows)),
        out_shape=jax.ShapeDtypeStruct(
            (col_count, own_freqs, shard_rows, columns_own), jnp.bfloat16
        ),
        in_specs=[VMEM] * (1 + row_count),
        out_specs=VMEM,
        name="second",
    )(tiles, *[middles[k] for k in range(row_count)])
    second = lax.all_to_all(second, "col", split_axis=0, concat_axis=0, tiled=True)
    second = second.reshape(
        col_count // splits, splits, own_freqs, shard_rows, columns_own
    ).transpose(3, 0, 2, 1, 4)
    second = second.reshape(shard_rows, local_freqs, columns_wide).astype(jnp.float32)
    return columns.astype(jnp.float32)[:, None, :] + damping * second


def solution(mesh):
    placed = (P(("col", "row"), "tm"), P(("col", "row"), "tm"), P(), P(), P(("col", "row"), None))
    return jax.shard_map(
        shards, mesh=mesh, in_specs=placed, out_specs=P(("col", "row"), "tm", None), check_vma=False
    )
```

```python
import functools

import jax
import jax.numpy as jnp
import numpy as np
from jax import lax
from jax.experimental import pallas as pl
from jax.experimental.pallas import tpu as pltpu
from jax.sharding import PartitionSpec as P

NT = 16
NF = 16

damping = 0.3

FULL = pltpu.CompilerParams(vmem_limit_bytes=67043328)
HBM = pl.BlockSpec(memory_space=pltpu.HBM)
VMEM = pl.BlockSpec(memory_space=pltpu.VMEM)
SMEM = pl.BlockSpec(memory_space=pltpu.SMEM)


def time_tables(count_times, count_freqs):
    moments = np.float32(0.25) * (np.arange(count_times, dtype=np.float32) + np.float32(0.5))
    omegas = np.float32(0.4) * (np.arange(count_freqs, dtype=np.float32) + np.float32(0.5))
    cosine = np.float32(0.5) * np.cos(omegas[:, None] * moments[None, :])
    return (moments, cosine.astype(jnp.bfloat16))


def swap(value, axis, bit):
    size = lax.axis_size(axis)
    return lax.ppermute(value, axis, [(i, i ^ bit) for i in range(size)])


def shift(value, axis, step):
    size = lax.axis_size(axis)
    return lax.ppermute(value, axis, [(i, (i + step) % size) for i in range(size)])


def bits_of(count):
    return [1 << b for b in reversed(range(count.bit_length() - 1))]


def spread(pieces, axis, bit, slot):
    out = dict(pieces)
    for key, value in pieces.items():
        moved = list(key)
        moved[slot] ^= bit
        out[tuple(moved)] = swap(value, axis, bit)
    return out


def run_copies(copies, sem):
    copies = [pltpu.make_async_copy(a, b, sem) for a, b in copies]
    for copy in copies:
        copy.start()
    for copy in copies:
        copy.wait()


def tile_kernel(row_keys, groups, dims, mix, factors, *refs):
    (times, freqs, half, shard_rows, places) = dims
    row_pieces = refs[: len(row_keys)]
    pieces = refs[len(row_pieces) :][: places * len(groups)]
    out, rows, cols, scaled, spectral, sems, out_sem = refs[len(row_pieces) + len(pieces) :]
    tm, p = lax.axis_index("tm"), lax.axis_index("col")
    part = cols.shape[2]
    copies = []
    for n in range(places):
        for i, kts in enumerate(groups):
            ref = pieces[n * len(groups) + i]
            for m, (kt, arr) in enumerate((kt, arr) for kt in kts for arr in range(2)):
                lane = pl.multiple_of((tm ^ kt) * half, half)
                to = cols.at[arr, n, :, pl.ds(lane, half)]
                copies.append((ref.at[:, pl.ds(m * half, half)], to))
    for (arr, kt, kc), ref in zip(row_keys, row_pieces):
        to = pl.multiple_of((p ^ kc) * shard_rows, shard_rows)
        lane = pl.multiple_of((tm ^ kt) * half, half)
        copies.append((ref, rows.at[arr, pl.ds(to, shard_rows), pl.ds(lane, half)]))
    run_copies(copies, sems)
    block = mix.shape[0] // freqs
    span = block * times

    for n in range(places):
        greens = []
        slot = n % scaled.shape[0]
        for arr in range(2):
            for g in range(part // block):
                values = cols[arr, n, pl.ds(g * block, block), :].astype(jnp.float32)
                for j in range(times):
                    factor = factors[arr, pl.ds(j, 1), :]
                    scaled[slot, arr, pl.ds(g * span + j * block, block), :] = (values * factor).astype(
                        jnp.bfloat16
                    )
            greens.append(
                lax.dot_general(
                    scaled[slot, arr],
                    rows[arr],
                    (((1,), (1,)), ((), ())),
                    preferred_element_type=jnp.float32,
                )
            )
        polar = (-2.0 * greens[0] * greens[1]).astype(jnp.bfloat16)
        for g in range(part // block):
            total = jnp.dot(
                mix[...], polar[g * span : (g + 1) * span], preferred_element_type=jnp.float32
            )
            spectral[n, :, pl.ds(g * block, block), :] = total.astype(jnp.bfloat16).reshape(
                freqs, block, total.shape[1]
            )
        pltpu.make_async_copy(spectral.at[n], out.at[:, n], out_sem.at[n]).start()
    for n in range(places):
        pltpu.make_async_copy(spectral.at[n], out.at[:, n], out_sem.at[n]).wait()


def pick_kernel(lanes, *refs):
    pieces, out, sem = refs[:-2], refs[-2], refs[-1]
    run_copies(
        [(ref.at[:, pl.ds(lanes, out.shape[2])], out.at[n]) for n, ref in enumerate(pieces)], sem
    )


def columns_kernel(keys, dims, *refs):
    (tm_count, row_count, col_count, shard_rows, part) = dims
    pieces = refs[: len(keys)]
    out, own, gathered, own_rows, sem = refs[len(keys) :]
    p = lax.axis_index("col")
    width = row_count * part
    copies = []
    wide = own.shape[0]
    for kc, ref in zip(keys, pieces):
        for kq in range(row_count):
            for t in range(tm_count):
                source = ref.at[kq, :, pl.ds(t * wide, wide)]
                to = pl.multiple_of((t * col_count + (p ^ kc)) * width + kq * part, part)
                copies.append((source, gathered.at[pl.ds(to, part), :]))
                if kq == 0:
                    to = pl.multiple_of((p ^ kc) * shard_rows + t * part, part)
                    copies.append((source, own_rows.at[pl.ds(to, part), :]))
    run_copies(copies, sem)
    out[...] = gathered[...].astype(jnp.float32).T.astype(jnp.bfloat16)
    own[...] = own_rows[...].astype(jnp.float32).T.astype(jnp.bfloat16)


def first_kernel(all_columns, own, tiles, out):
    sources, freqs, width, rows = tiles.shape
    for k in range(freqs):
        weights = tiles[:, k].reshape(sources * width, rows)
        first = jnp.dot(all_columns[...], weights, preferred_element_type=jnp.float32)
        out[k] = (own[...].astype(jnp.float32) + damping * first).astype(jnp.bfloat16)


def second_kernel(dims, tiles, *refs):
    (tm_count, row_count, col_count, part, shard_rows) = dims
    middles = refs[:row_count]
    out = refs[row_count]
    _, freqs, _, _ = tiles.shape
    for k in range(freqs):
        total = None
        for kq in range(row_count):
            weights = jnp.concatenate(
                [
                    tiles[t * col_count + p, k, pl.ds(kq * part, part), :]
                    for p in range(col_count)
                    for t in range(tm_count)
                ],
                axis=0,
            )
            term = jnp.dot(middles[kq][k], weights, preferred_element_type=jnp.float32)
            total = term if total is None else total + term
        second = total.T.astype(jnp.bfloat16)
        for p in range(col_count):
            out[p, k] = second[p * shard_rows : (p + 1) * shard_rows]


def shards(occ_orbitals, empty_orbitals, occ_rate, empty_rate, columns):
    tm_count, row_count, col_count = (lax.axis_size(a) for a in ("tm", "row", "col"))
    shard_rows, half = occ_orbitals.shape
    columns_wide = columns.shape[1]
    orbitals = tm_count * half
    part = shard_rows // tm_count
    width = row_count * part
    tile_rows = col_count * shard_rows
    tm_index, col_index = lax.axis_index("tm"), lax.axis_index("col")
    both = (occ_orbitals, empty_orbitals)
    high, low = bits_of(col_count)[:-1], bits_of(col_count)[-1:]

    rows_of = [{(arr, 0, 0): value} for arr, value in enumerate(both)]
    own = jnp.concatenate(
        [lax.dynamic_slice_in_dim(value, tm_index * part, part, 0) for value in both]
        + [columns[t * part : (t + 1) * part] for t in range(tm_count)],
        axis=1,
    )
    for bit in bits_of(tm_count):
        rows_of = [spread(pieces, "tm", bit, 1) for pieces in rows_of]
    near = [{k: v for k, v in pieces.items() if k[1] == 0} for pieces in rows_of]
    far = [{k: v for k, v in pieces.items() if k[1] != 0} for pieces in rows_of]
    for bit in high:
        near = [spread(pieces, "col", bit, 2) for pieces in near]
    got = [
        lax.dynamic_slice_in_dim(far[arr][(arr, kt, 0)], tm_index * part, part, 0)
        for kt in range(1, tm_count)
        for arr in range(2)
    ]
    streams, late = (0,), tuple(range(1, tm_count))
    cols_of = {(0, streams): own, (0, late): jnp.concatenate(got, axis=1)}

    def ring_step(group, source, target, step):
        cols_of[(target, group)] = shift(cols_of[(source, group)], "row", step)

    behind = (row_count - 1) // 2
    ahead = row_count // 2
    ring_step(streams, 0, 1, -1)
    if behind:
        ring_step(streams, 0, row_count - 1, 1)
    for bit in high:
        far = [spread(pieces, "col", bit, 2) for pieces in far]
    if behind:
        ring_step(late, 0, row_count - 1, 1)
    ring_step(late, 0, 1, -1)
    for k in range(2, ahead + 1):
        ring_step(streams, k - 1, k, -1)
    for k in range(2, behind + 1):
        ring_step(streams, row_count - k + 1, row_count - k, 1)
    for bit in low:
        near = [spread(pieces, "col", bit, 2) for pieces in near]
    for k in range(2, ahead + 1):
        ring_step(late, k - 1, k, -1)
    for k in range(2, behind + 1):
        ring_step(late, row_count - k + 1, row_count - k, 1)
    for bit in low:
        far = [spread(pieces, "col", bit, 2) for pieces in far]
    row_pieces = {**near[0], **near[1], **far[0], **far[1]}
    row_keys = list(row_pieces)

    picked = pl.pallas_call(
        functools.partial(pick_kernel, 2 * half),
        out_shape=jax.ShapeDtypeStruct((row_count, part, tm_count * columns_wide), jnp.bfloat16),
        in_specs=[HBM] * row_count,
        out_specs=VMEM,
        scratch_shapes=[pltpu.SemaphoreType.DMA],
        compiler_params=FULL,
        name="pick",
    )(*[cols_of[(kq, streams)] for kq in range(row_count)])
    column_pieces = {(0,): picked}
    for bit in high:
        column_pieces = spread(column_pieces, "col", bit, 0)
    for bit in low:
        column_pieces = spread(column_pieces, "col", bit, 0)

    moments, cosine = time_tables(NT, NF)
    factors = jnp.exp(-jnp.stack([occ_rate, empty_rate])[:, None, :] * moments[None, :, None])
    block = min(16, part)
    mix = jnp.asarray(np.kron(cosine.astype(np.float32), np.eye(block)).astype(jnp.bfloat16))
    groups = [streams, late]
    pieces = [cols_of[(place, kts)] for place in range(row_count) for kts in groups]
    tile = pl.pallas_call(
        functools.partial(
            tile_kernel, row_keys, groups, (NT, NF, half, shard_rows, row_count)
        ),
        out_shape=jax.ShapeDtypeStruct((NF, row_count, part, tile_rows), jnp.bfloat16),
        in_specs=[VMEM, VMEM] + [HBM] * (len(row_keys) + len(pieces)),
        out_specs=HBM,
        scratch_shapes=[
            pltpu.VMEM((2, tile_rows, orbitals), jnp.bfloat16),
            pltpu.VMEM((2, row_count, part, orbitals), jnp.bfloat16),
            pltpu.VMEM((2, 2, NT * part, orbitals), jnp.bfloat16),
            pltpu.VMEM((row_count, NF, part, tile_rows), jnp.bfloat16),
            pltpu.SemaphoreType.DMA,
            pltpu.SemaphoreType.DMA((row_count,)),
        ],
        compiler_params=FULL,
        name="tile",
    )(mix, factors, *[row_pieces[k] for k in row_keys], *pieces)

    keys = [key[0] for key in column_pieces]
    all_columns, own_columns = pl.pallas_call(
        functools.partial(columns_kernel, keys, (tm_count, row_count, col_count, shard_rows, part)),
        out_shape=(
            jax.ShapeDtypeStruct((columns_wide, tm_count * col_count * width), jnp.bfloat16),
            jax.ShapeDtypeStruct((columns_wide, tile_rows), jnp.bfloat16),
        ),
        in_specs=[HBM] * len(keys),
        out_specs=(VMEM, VMEM),
        scratch_shapes=[
            pltpu.VMEM((tm_count * col_count * width, columns_wide), jnp.bfloat16),
            pltpu.VMEM((tile_rows, columns_wide), jnp.bfloat16),
            pltpu.SemaphoreType.DMA,
        ],
        compiler_params=FULL,
        name="columns",
    )(*column_pieces.values())

    local_freqs = NF // tm_count
    own_freqs = max(1, local_freqs // col_count)
    splits = max(1, col_count // local_freqs)
    columns_own = columns_wide // splits
    sent = tile.reshape(NF // own_freqs, own_freqs, width, tile_rows)
    if splits > 1:
        sent = jnp.repeat(sent, splits, axis=0)
        first_row = (col_index % splits) * columns_own
        all_columns = lax.dynamic_slice_in_dim(all_columns, first_row, columns_own, 0)
        own_columns = lax.dynamic_slice_in_dim(own_columns, first_row, columns_own, 0)
    tiles = lax.all_to_all(sent, ("tm", "col"), split_axis=0, concat_axis=0, tiled=True)

    middle = pl.pallas_call(
        first_kernel,
        out_shape=jax.ShapeDtypeStruct((own_freqs, columns_own, tile_rows), jnp.bfloat16),
        in_specs=[VMEM, VMEM, VMEM],
        out_specs=VMEM,
        name="first",
    )(all_columns, own_columns, tiles)
    middles = {0: middle}
    middles[1] = shift(middle, "row", -1)
    for k in range(1, behind + 1):
        middles[row_count - k] = shift(middles[(row_count - k + 1) % row_count], "row", 1)
    for k in range(2, ahead + 1):
        middles[k] = shift(middles[k - 1], "row", -1)
    second = pl.pallas_call(
        functools.partial(second_kernel, (tm_count, row_count, col_count, part, shard_rows)),
        out_shape=jax.ShapeDtypeStruct(
            (col_count, own_freqs, shard_rows, columns_own), jnp.bfloat16
        ),
        in_specs=[VMEM] * (1 + row_count),
        out_specs=VMEM,
        name="second",
    )(tiles, *[middles[k] for k in range(row_count)])
    second = lax.all_to_all(second, "col", split_axis=0, concat_axis=0, tiled=True)
    second = second.reshape(
        col_count // splits, splits, own_freqs, shard_rows, columns_own
    ).transpose(3, 0, 2, 1, 4)
    second = second.reshape(shard_rows, local_freqs, columns_wide).astype(jnp.float32)
    return columns.astype(jnp.float32)[:, None, :] + damping * second


def solution(mesh):
    placed = (P(("col", "row"), "tm"), P(("col", "row"), "tm"), P(), P(), P(("col", "row"), None))
    return jax.shard_map(
        shards, mesh=mesh, in_specs=placed, out_specs=P(("col", "row"), "tm", None), check_vma=False
    )
```

```python
import functools

import jax
import jax.numpy as jnp
import numpy as np
from jax import lax
from jax.experimental import pallas as pl
from jax.experimental.pallas import tpu as pltpu
from jax.sharding import PartitionSpec as P

NT = 16
NF = 16

damping = 0.3

FULL = pltpu.CompilerParams(vmem_limit_bytes=67043328)
HBM = pl.BlockSpec(memory_space=pltpu.HBM)
VMEM = pl.BlockSpec(memory_space=pltpu.VMEM)
SMEM = pl.BlockSpec(memory_space=pltpu.SMEM)


def time_tables(count_times, count_freqs):
    moments = np.float32(0.25) * (np.arange(count_times, dtype=np.float32) + np.float32(0.5))
    omegas = np.float32(0.4) * (np.arange(count_freqs, dtype=np.float32) + np.float32(0.5))
    cosine = np.float32(0.5) * np.cos(omegas[:, None] * moments[None, :])
    return (moments, cosine.astype(jnp.bfloat16))


def swap(value, axis, bit):
    size = lax.axis_size(axis)
    return lax.ppermute(value, axis, [(i, i ^ bit) for i in range(size)])


def shift(value, axis, step):
    size = lax.axis_size(axis)
    return lax.ppermute(value, axis, [(i, (i + step) % size) for i in range(size)])


def bits_of(count):
    return [1 << b for b in reversed(range(count.bit_length() - 1))]


def spread(pieces, axis, bit, slot):
    out = dict(pieces)
    for key, value in pieces.items():
        moved = list(key)
        moved[slot] ^= bit
        out[tuple(moved)] = swap(value, axis, bit)
    return out


def run_copies(copies, sem):
    copies = [pltpu.make_async_copy(a, b, sem) for a, b in copies]
    for copy in copies:
        copy.start()
    for copy in copies:
        copy.wait()


def copies_of(pairs, sem):
    copies = [pltpu.make_async_copy(a, b, sem) for a, b in pairs]
    for copy in copies:
        copy.start()
    return copies


def wait_for(copies):
    for copy in copies:
        copy.wait()


def tile_kernel(row_keys, groups, dims, mix, occ_rate, empty_rate, *refs):
    (times, freqs, half, shard_rows, places, col_count, own_freqs, splits) = dims
    row_pieces = refs[: len(row_keys)]
    pieces = refs[len(row_pieces) :][: places * len(groups)]
    rest = refs[len(row_pieces) + len(pieces) :]
    outs, (rows, cols, scaled, greens, factors, spectral, sems, out_sem) = rest[:-8], rest[-8:]
    tm, p = lax.axis_index("tm"), lax.axis_index("col")
    part = cols.shape[2]
    local_freqs = freqs // (len(outs) // col_count)
    pairs = [[], []]
    for n in range(places):
        for i, kts in enumerate(groups):
            ref = pieces[n * len(groups) + i]
            for m, (kt, arr) in enumerate((kt, arr) for kt in kts for arr in range(2)):
                lane = pl.multiple_of((tm ^ kt) * half, half)
                to = cols.at[arr, n, :, pl.ds(lane, half)]
                pairs[arr].append((ref.at[:, pl.ds(m * half, half)], to))
    for (arr, kt, kc), ref in zip(row_keys, row_pieces):
        to = pl.multiple_of((p ^ kc) * shard_rows, shard_rows)
        lane = pl.multiple_of((tm ^ kt) * half, half)
        pairs[arr].append((ref, rows.at[arr, pl.ds(to, shard_rows), pl.ds(lane, half)]))
    arriving = [copies_of(pairs[arr], sems.at[arr]) for arr in range(2)]
    steps = lax.broadcasted_iota(jnp.int32, factors.shape[1:], 0).astype(jnp.float32)
    for arr, rate in enumerate((occ_rate, empty_rate)):
        factors[arr] = jnp.exp(-rate[...] * (0.25 * (steps + 0.5)))
    block = mix.shape[0] // freqs
    span = block * times

    def green(arr, n):
        slot = (arr * places + n) % scaled.shape[0]
        for g in range(part // block):
            values = cols[arr, n, pl.ds(g * block, block), :].astype(jnp.float32)
            for j in range(times):
                factor = factors[arr, pl.ds(j, 1), :]
                scaled[slot, pl.ds(g * span + j * block, block), :] = (values * factor).astype(
                    jnp.bfloat16
                )
        return lax.dot_general(
            scaled[slot], rows[arr], (((1,), (1,)), ((), ())), preferred_element_type=jnp.float32
        )

    wait_for(arriving[0])
    for n in range(places):
        greens[n] = -2.0 * green(0, n)
    wait_for(arriving[1])
    for n in range(places):
        polar = (greens[n] * green(1, n)).astype(jnp.bfloat16)
        for g in range(part // block):
            total = jnp.dot(
                mix[...], polar[g * span : (g + 1) * span], preferred_element_type=jnp.float32
            )
            spectral[n, :, pl.ds(g * block, block), :] = total.astype(jnp.bfloat16).reshape(
                freqs, block, total.shape[1]
            )
        if len(outs) <= 8 or n == places - 1:
            done = slice(n, n + 1) if len(outs) <= 8 else slice(0, places)
            leaving = leaving if n else []
            for r, ref in enumerate(outs):
                to_tm, to_col = tm ^ (r // col_count), p ^ (r % col_count)
                start = to_tm * local_freqs + (to_col // splits) * own_freqs
                pairs = [
                    (spectral.at[m, pl.ds(start, own_freqs)], ref.at[:, m])
                    for m in range(places)[done]
                ]
                leaving += copies_of(pairs, out_sem)
        else:
            leaving = []
    wait_for(leaving)


def pack_kernel(dims, occ, empty, columns, own, other, sem):
    (part, half, tm_count) = dims
    tm = lax.axis_index("tm")
    wide = columns.shape[1]
    pairs = []
    for arr, ref in enumerate((occ, empty)):
        for kt in range(tm_count):
            source = ref.at[pl.ds(pl.multiple_of((tm ^ kt) * part, part), part), :]
            lanes = pl.ds(arr * half, half)
            pairs.append((source, other.at[kt - 1, :, lanes] if kt else own.at[:, lanes]))
    for t in range(tm_count):
        lanes = pl.ds(2 * half + t * wide, wide)
        pairs.append((columns.at[pl.ds(t * part, part), :], own.at[:, lanes]))
    wait_for(copies_of(pairs, sem))


def pick_kernel(lanes, *refs):
    pieces, out, sem = refs[:-2], refs[-2], refs[-1]
    run_copies(
        [(ref.at[:, pl.ds(lanes, out.shape[2])], out.at[n]) for n, ref in enumerate(pieces)], sem
    )


def columns_kernel(keys, dims, *refs):
    (tm_count, row_count, col_count, shard_rows, part) = dims
    pieces = refs[: len(keys)]
    out, own, gathered, own_rows, sem = refs[len(keys) :]
    p = lax.axis_index("col")
    width = row_count * part
    copies = []
    wide = own.shape[0]
    for kc, ref in zip(keys, pieces):
        for kq in range(row_count):
            for t in range(tm_count):
                source = ref.at[kq, :, pl.ds(t * wide, wide)]
                to = pl.multiple_of((t * col_count + (p ^ kc)) * width + kq * part, part)
                copies.append((source, gathered.at[pl.ds(to, part), :]))
                if kq == 0:
                    to = pl.multiple_of((p ^ kc) * shard_rows + t * part, part)
                    copies.append((source, own_rows.at[pl.ds(to, part), :]))
    run_copies(copies, sem)
    out[...] = gathered[...].astype(jnp.float32).T.astype(jnp.bfloat16)
    own[...] = own_rows[...].astype(jnp.float32).T.astype(jnp.bfloat16)


def source_of(r, col_count):
    tm, p = lax.axis_index("tm"), lax.axis_index("col")
    return (tm ^ (r // col_count)) * col_count + (p ^ (r % col_count))


def first_kernel(col_count, all_columns, own, *refs):
    columns_v, own_v, tiles_v, middle_v, sems = refs[-5:]
    (freqs, sources, places, part, rows) = tiles_v.shape
    tiles, outs = refs[:sources], refs[sources : sources + freqs]
    arriving = [copies_of([(all_columns, columns_v), (own, own_v)], sems.at[freqs])]
    arriving += [
        copies_of(
            [
                (ref.at[k], tiles_v.at[k, source_of(r, col_count)])
                for r, ref in enumerate(tiles)
            ],
            sems.at[k],
        )
        for k in range(freqs)
    ]
    wait_for(arriving[0])
    leaving = []
    for k in range(freqs):
        wait_for(arriving[1 + k])
        weights = tiles_v[k].reshape(sources * places * part, rows)
        first = jnp.dot(columns_v[...], weights, preferred_element_type=jnp.float32)
        middle_v[k] = (own_v[...].astype(jnp.float32) + damping * first).astype(jnp.bfloat16)
        leaving += copies_of([(middle_v.at[k], outs[k])], sems.at[freqs + 1])
    wait_for(leaving)


def weights_of(tiles_v, k, index, dims):
    (tm_count, col_count) = dims
    return jnp.concatenate(
        [tiles_v[t * col_count + p, k, index] for p in range(col_count) for t in range(tm_count)],
        axis=0,
    )


def near_kernel(dims, *refs):
    (tm_count, col_count, places) = dims
    sources, count = tm_count * col_count, len(places)
    (out, tiles_v, middles_v, total_v, sems) = refs[-5:]
    tiles, middles = refs[:sources], refs[sources:-5]
    freqs = total_v.shape[0]
    arriving = copies_of(
        [
            (ref.at[:, place], tiles_v.at[source_of(r, col_count), :, n])
            for n, place in enumerate(places)
            for r, ref in enumerate(tiles)
        ],
        sems.at[0],
    )
    arriving += copies_of(
        [(ref, middles_v.at[i // freqs, i % freqs]) for i, ref in enumerate(middles)], sems.at[0]
    )
    wait_for(arriving)
    for k in range(freqs):
        total = None
        for n in range(count):
            weights = weights_of(tiles_v, k, n, dims[:2])
            term = jnp.dot(middles_v[n, k], weights, preferred_element_type=jnp.float32)
            total = term if total is None else total + term
        total_v[k] = total
    wait_for(copies_of([(total_v, out)], sems.at[1]))


def far_kernel(dims, *refs):
    (tm_count, col_count, place, top, shard_rows, other) = dims
    sources = tm_count * col_count
    tiles, total, rest = refs[:sources], refs[sources], refs[sources + 1 :]
    middles, outs = rest[: -5 - top], rest[-5 - top : -5]
    (tiles_v, total_v, middle_v, second_v, sems) = rest[-5:]
    p = lax.axis_index("col")
    freqs = total_v.shape[0]
    span = top * shard_rows
    part_of = p // top
    lane = pl.multiple_of((1 - part_of if other else part_of) * span, span)
    pairs = [
        (ref.at[:, place, :, pl.ds(lane, span)], tiles_v.at[source_of(r, col_count), :, 0])
        for r, ref in enumerate(tiles)
    ]
    pairs += [(total.at[:, :, pl.ds(lane, span)], total_v)]
    pairs += [(ref, middle_v.at[k]) for k, ref in enumerate(middles)]
    wait_for(copies_of(pairs, sems.at[0]))
    for k in range(freqs):
        weights = weights_of(tiles_v, k, 0, dims[:2])
        term = jnp.dot(middle_v[k], weights, preferred_element_type=jnp.float32)
        second = (total_v[k] + term).T.astype(jnp.bfloat16)
        for i in range(top):
            second_v[i, k] = second[i * shard_rows : (i + 1) * shard_rows]
    slot = lax.rem(p, top)
    wait_for(copies_of([(second_v.at[slot ^ d], ref) for d, ref in enumerate(outs)], sems.at[1]))


def final_kernel(keys, splits, columns, *refs):
    pieces, (out, held, columns_v, out_v, sems) = refs[: len(keys)], refs[len(keys) :]
    p = lax.axis_index("col")
    pairs = [(ref, held.at[p ^ k]) for k, ref in zip(keys, pieces)] + [(columns, columns_v)]
    wait_for(copies_of(pairs, sems.at[0]))
    (count, freqs, shard_rows, wide) = held.shape
    step = max(16, shard_rows // 2)
    leaving = []
    for start in range(0, shard_rows, step):
        rows = slice(start, start + step)
        base = columns_v[rows].astype(jnp.float32)
        for source in range(count):
            lane = (source % splits) * wide
            for k in range(freqs):
                value = base[:, lane : lane + wide] + damping * held[source, k, rows].astype(
                    jnp.float32
                )
                out_v[rows, (source // splits) * freqs + k, lane : lane + wide] = value
        leaving += copies_of([(out_v.at[rows], out.at[rows])], sems.at[1])
    wait_for(leaving)


def shards(occ_orbitals, empty_orbitals, occ_rate, empty_rate, columns):
    tm_count, row_count, col_count = (lax.axis_size(a) for a in ("tm", "row", "col"))
    shard_rows, half = occ_orbitals.shape
    columns_wide = columns.shape[1]
    orbitals = tm_count * half
    part = shard_rows // tm_count
    width = row_count * part
    tile_rows = col_count * shard_rows
    col_index = lax.axis_index("col")
    both = (occ_orbitals, empty_orbitals)
    sources = tm_count * col_count
    local_freqs = NF // tm_count
    own_freqs = max(1, local_freqs // col_count)
    splits = max(1, col_count // local_freqs)
    columns_own = columns_wide // splits
    high, low = bits_of(col_count)[:-1], bits_of(col_count)[-1:]

    rows_of = [{(arr, 0, 0): value} for arr, value in enumerate(both)]
    own, other = pl.pallas_call(
        functools.partial(pack_kernel, (part, half, tm_count)),
        out_shape=(
            jax.ShapeDtypeStruct((part, 2 * half + tm_count * columns_wide), jnp.bfloat16),
            jax.ShapeDtypeStruct((tm_count - 1, part, 2 * half), jnp.bfloat16),
        ),
        in_specs=[HBM] * 3,
        out_specs=(VMEM, VMEM),
        scratch_shapes=[pltpu.SemaphoreType.DMA],
        compiler_params=FULL,
        name="pack",
    )(occ_orbitals, empty_orbitals, columns)
    got = [
        swap(other[kt - 1], "tm", kt) if tm_count > 2 else swap(other.reshape(part, -1), "tm", kt)
        for kt in range(1, tm_count)
    ]
    for bit in bits_of(tm_count):
        rows_of = [spread(pieces, "tm", bit, 1) for pieces in rows_of]
    near = [{k: v for k, v in pieces.items() if k[1] == 0} for pieces in rows_of]
    far = [{k: v for k, v in pieces.items() if k[1] != 0} for pieces in rows_of]
    for bit in high:
        near = [spread(pieces, "col", bit, 2) for pieces in near]
    streams, late = (0,), tuple(range(1, tm_count))
    cols_of = {(0, streams): own, (0, late): jnp.concatenate(got, axis=1) if len(got) > 1 else got[0]}

    def ring_step(group, source, target, step):
        cols_of[(target, group)] = shift(cols_of[(source, group)], "row", step)

    behind = (row_count - 1) // 2
    ahead = row_count // 2
    ring_step(streams, 0, 1, -1)
    if behind:
        ring_step(streams, 0, row_count - 1, 1)
    for bit in high:
        far = [spread(pieces, "col", bit, 2) for pieces in far]
    if behind:
        ring_step(late, 0, row_count - 1, 1)
    ring_step(late, 0, 1, -1)
    for k in range(2, ahead + 1):
        ring_step(streams, k - 1, k, -1)
    for k in range(2, behind + 1):
        ring_step(streams, row_count - k + 1, row_count - k, 1)
    for bit in low:
        near = [spread(pieces, "col", bit, 2) for pieces in near]
    for k in range(2, ahead + 1):
        ring_step(late, k - 1, k, -1)
    for k in range(2, behind + 1):
        ring_step(late, row_count - k + 1, row_count - k, 1)
    for bit in low:
        far = [spread(pieces, "col", bit, 2) for pieces in far]
    row_pieces = {**near[0], **near[1], **far[0], **far[1]}
    row_keys = list(row_pieces)

    picked = pl.pallas_call(
        functools.partial(pick_kernel, 2 * half),
        out_shape=jax.ShapeDtypeStruct((row_count, part, tm_count * columns_wide), jnp.bfloat16),
        in_specs=[HBM] * row_count,
        out_specs=VMEM,
        scratch_shapes=[pltpu.SemaphoreType.DMA],
        compiler_params=FULL,
        name="pick",
    )(*[cols_of[(kq, streams)] for kq in range(row_count)])
    column_pieces = {(0,): picked}
    for bit in high:
        column_pieces = spread(column_pieces, "col", bit, 0)
    for bit in low:
        column_pieces = spread(column_pieces, "col", bit, 0)

    cosine = time_tables(NT, NF)[1]
    rates = [rate.reshape(1, -1) for rate in (occ_rate, empty_rate)]
    block = min(16, part)
    mix = jnp.asarray(np.kron(cosine.astype(np.float32), np.eye(block)).astype(jnp.bfloat16))
    groups = [streams, late]
    pieces = [cols_of[(place, kts)] for place in range(row_count) for kts in groups]
    sent = pl.pallas_call(
        functools.partial(
            tile_kernel,
            row_keys,
            groups,
            (NT, NF, half, shard_rows, row_count, col_count, own_freqs, splits),
        ),
        out_shape=[
            jax.ShapeDtypeStruct((own_freqs, row_count, part, tile_rows), jnp.bfloat16)
        ]
        * sources,
        in_specs=[VMEM] * 3 + [HBM] * (len(row_keys) + len(pieces)),
        out_specs=[HBM] * sources,
        scratch_shapes=[
            pltpu.VMEM((2, tile_rows, orbitals), jnp.bfloat16),
            pltpu.VMEM((2, row_count, part, orbitals), jnp.bfloat16),
            pltpu.VMEM((2, NT * part, orbitals), jnp.bfloat16),
            pltpu.VMEM((row_count, NT * part, tile_rows), jnp.float32),
            pltpu.VMEM((2, NT, orbitals), jnp.float32),
            pltpu.VMEM((row_count, NF, part, tile_rows), jnp.bfloat16),
            pltpu.SemaphoreType.DMA((2,)),
            pltpu.SemaphoreType.DMA,
        ],
        compiler_params=FULL,
        name="tile",
    )(mix, *rates, *[row_pieces[k] for k in row_keys], *pieces)

    keys = [key[0] for key in column_pieces]
    all_columns, own_columns = pl.pallas_call(
        functools.partial(columns_kernel, keys, (tm_count, row_count, col_count, shard_rows, part)),
        out_shape=(
            jax.ShapeDtypeStruct((columns_wide, tm_count * col_count * width), jnp.bfloat16),
            jax.ShapeDtypeStruct((columns_wide, tile_rows), jnp.bfloat16),
        ),
        in_specs=[HBM] * len(keys),
        out_specs=(VMEM, VMEM),
        scratch_shapes=[
            pltpu.VMEM((tm_count * col_count * width, columns_wide), jnp.bfloat16),
            pltpu.VMEM((tile_rows, columns_wide), jnp.bfloat16),
            pltpu.SemaphoreType.DMA,
        ],
        compiler_params=FULL,
        name="columns",
    )(*column_pieces.values())

    if splits > 1:
        first_row = (col_index % splits) * columns_own
        all_columns = lax.dynamic_slice_in_dim(all_columns, first_row, columns_own, 0)
        own_columns = lax.dynamic_slice_in_dim(own_columns, first_row, columns_own, 0)
    far_first = sorted(range(1, sources), key=lambda r: -(r >= col_count) - (r % col_count > 1))
    tiles = [sent[0]] * sources
    for r in far_first:
        pairs = [(i, i ^ r) for i in range(sources)]
        tiles[r] = lax.ppermute(sent[r], ("tm", "col"), pairs)

    first_shape = (own_freqs, columns_own, tile_rows)
    middle = pl.pallas_call(
        functools.partial(first_kernel, col_count),
        out_shape=[jax.ShapeDtypeStruct(first_shape[1:], jnp.bfloat16)] * own_freqs,
        in_specs=[HBM] * (2 + sources),
        out_specs=[HBM] * own_freqs,
        scratch_shapes=[
            pltpu.VMEM((columns_own, sources * width), jnp.bfloat16),
            pltpu.VMEM((columns_own, tile_rows), jnp.bfloat16),
            pltpu.VMEM((own_freqs, sources, row_count, part, tile_rows), jnp.bfloat16),
            pltpu.VMEM(first_shape, jnp.bfloat16),
            pltpu.SemaphoreType.DMA((own_freqs + 2,)),
        ],
        compiler_params=FULL,
        name="first",
    )(all_columns, own_columns, *tiles)
    middles = {(0, k): value for k, value in enumerate(middle)}

    def middle_step(source, target, step):
        for k in range(own_freqs):
            middles[(target, k)] = shift(middles[(source, k)], "row", step)

    middle_step(0, 1, -1)
    for k in range(1, behind + 1):
        middle_step((row_count - k + 1) % row_count, row_count - k, 1)
    for k in range(2, ahead + 1):
        middle_step(k - 1, k, -1)
    own_range = range(own_freqs)
    last = ahead
    places = [k for k in range(row_count) if k != last]
    total = pl.pallas_call(
        functools.partial(near_kernel, (tm_count, col_count, places)),
        out_shape=jax.ShapeDtypeStruct(first_shape, jnp.float32),
        in_specs=[HBM] * (sources + len(places) * own_freqs),
        out_specs=HBM,
        scratch_shapes=[
            pltpu.VMEM((sources, own_freqs, len(places), part, tile_rows), jnp.bfloat16),
            pltpu.VMEM((len(places),) + first_shape, jnp.bfloat16),
            pltpu.VMEM(first_shape, jnp.float32),
            pltpu.SemaphoreType.DMA((2,)),
        ],
        compiler_params=FULL,
        name="near",
    )(*tiles, *[middles[(place, k)] for place in places for k in own_range])
    top = col_count // 2
    span = top * shard_rows
    seconds = []
    for other in (True, False):
        seconds.append(
            pl.pallas_call(
                functools.partial(far_kernel, (tm_count, col_count, last, top, shard_rows, other)),
                out_shape=[jax.ShapeDtypeStruct((own_freqs, shard_rows, columns_own), jnp.bfloat16)]
                * top,
                in_specs=[HBM] * (sources + 1 + own_freqs),
                out_specs=[HBM] * top,
                scratch_shapes=[
                    pltpu.VMEM((sources, own_freqs, 1, part, span), jnp.bfloat16),
                    pltpu.VMEM((own_freqs, columns_own, span), jnp.float32),
                    pltpu.VMEM(first_shape, jnp.bfloat16),
                    pltpu.VMEM((top, own_freqs, shard_rows, columns_own), jnp.bfloat16),
                    pltpu.SemaphoreType.DMA((2,)),
                ],
                compiler_params=FULL,
            )(*tiles, total, *[middles[(last, k)] for k in own_range])
        )
    parts = {0: seconds[1][0]}
    for group, start in ((seconds[0], top), (seconds[1], 0)):
        for d, value in enumerate(group):
            if start + d:
                parts[start + d] = swap(value, "col", start + d)
    return pl.pallas_call(
        functools.partial(final_kernel, list(parts), splits),
        out_shape=jax.ShapeDtypeStruct((shard_rows, local_freqs, columns_wide), jnp.float32),
        in_specs=[HBM] * (1 + len(parts)),
        out_specs=HBM,
        scratch_shapes=[
            pltpu.VMEM((col_count, own_freqs, shard_rows, columns_own), jnp.bfloat16),
            pltpu.VMEM((shard_rows, columns_wide), jnp.bfloat16),
            pltpu.VMEM((shard_rows, local_freqs, columns_wide), jnp.float32),
            pltpu.SemaphoreType.DMA((2,)),
        ],
        compiler_params=FULL,
        name="final",
    )(columns, *parts.values())


def solution(mesh):
    placed = (P(("col", "row"), "tm"), P(("col", "row"), "tm"), P(), P(), P(("col", "row"), None))
    return jax.shard_map(
        shards, mesh=mesh, in_specs=placed, out_specs=P(("col", "row"), "tm", None), check_vma=False
    )
```

```python
import functools

import jax
import jax.numpy as jnp
import numpy as np
from jax import lax
from jax.experimental import pallas as pl
from jax.experimental.pallas import tpu as pltpu
from jax.sharding import PartitionSpec as P

NT = 16
NF = 16

damping = 0.3

BATCH = 1

FULL = pltpu.CompilerParams(vmem_limit_bytes=67043328)
HBM = pl.BlockSpec(memory_space=pltpu.HBM)
VMEM = pl.BlockSpec(memory_space=pltpu.VMEM)
SMEM = pl.BlockSpec(memory_space=pltpu.SMEM)


def time_tables(count_times, count_freqs):
    moments = np.float32(0.25) * (np.arange(count_times, dtype=np.float32) + np.float32(0.5))
    omegas = np.float32(0.4) * (np.arange(count_freqs, dtype=np.float32) + np.float32(0.5))
    cosine = np.float32(0.5) * np.cos(omegas[:, None] * moments[None, :])
    return (moments, cosine.astype(jnp.bfloat16))


def swap(value, axis, bit):
    size = lax.axis_size(axis)
    return lax.ppermute(value, axis, [(i, i ^ bit) for i in range(size)])


def shift(value, axis, step):
    size = lax.axis_size(axis)
    return lax.ppermute(value, axis, [(i, (i + step) % size) for i in range(size)])


def bits_of(count):
    return [1 << b for b in reversed(range(count.bit_length() - 1))]


def spread(pieces, axis, bit, slot):
    out = dict(pieces)
    for key, value in pieces.items():
        moved = list(key)
        moved[slot] ^= bit
        out[tuple(moved)] = swap(value, axis, bit)
    return out


def run_copies(copies, sem):
    copies = [pltpu.make_async_copy(a, b, sem) for a, b in copies]
    for copy in copies:
        copy.start()
    for copy in copies:
        copy.wait()


def copies_of(pairs, sem):
    copies = [pltpu.make_async_copy(a, b, sem) for a, b in pairs]
    for copy in copies:
        copy.start()
    return copies


def wait_for(copies):
    for copy in copies:
        copy.wait()


def tile_kernel(row_keys, groups, dims, mix, occ_rate, empty_rate, *refs):
    (times, freqs, half, shard_rows, places, col_count, own_freqs, splits) = dims
    row_pieces = refs[: len(row_keys)]
    pieces = refs[len(row_pieces) :][: places * len(groups)]
    rest = refs[len(row_pieces) + len(pieces) :]
    outs, (rows, cols, scaled, factors, spectral, sems, out_sem) = rest[:-7], rest[-7:]
    tm, p = lax.axis_index("tm"), lax.axis_index("col")
    part = cols.shape[2]
    local_freqs = freqs // (len(outs) // col_count)
    pairs = [[], []]
    for n in range(places):
        for i, kts in enumerate(groups):
            ref = pieces[n * len(groups) + i]
            for m, (kt, arr) in enumerate((kt, arr) for kt in kts for arr in range(2)):
                lane = pl.multiple_of((tm ^ kt) * half, half)
                to = cols.at[arr, n, :, pl.ds(lane, half)]
                pairs[arr].append((ref.at[:, pl.ds(m * half, half)], to))
    for (arr, kt, kc), ref in zip(row_keys, row_pieces):
        to = pl.multiple_of((p ^ kc) * shard_rows, shard_rows)
        lane = pl.multiple_of((tm ^ kt) * half, half)
        pairs[arr].append((ref, rows.at[arr, pl.ds(to, shard_rows), pl.ds(lane, half)]))
    arriving = [copies_of(pairs[arr], sems.at[arr]) for arr in range(2)]
    steps = lax.broadcasted_iota(jnp.int32, factors.shape[1:], 0).astype(jnp.float32)
    for arr, rate in enumerate((occ_rate, empty_rate)):
        factors[arr] = jnp.exp(-rate[...] * (0.25 * (steps + 0.5)))
    block = mix.shape[0] // freqs
    span = block * times
    batch = scaled.shape[1] // (part * times)
    for first in range(0, places, batch):
        greens = []
        for arr in range(2):
            if first == 0:
                wait_for(arriving[arr])
            for m in range(batch):
                for g in range(part // block):
                    values = cols[arr, first + m, pl.ds(g * block, block), :].astype(jnp.float32)
                    start = m * part * times + g * span
                    for j in range(times):
                        factor = factors[arr, pl.ds(j, 1), :]
                        scaled[arr, pl.ds(start + j * block, block), :] = (values * factor).astype(
                            jnp.bfloat16
                        )
            greens.append(
                lax.dot_general(
                    scaled[arr],
                    rows[arr],
                    (((1,), (1,)), ((), ())),
                    preferred_element_type=jnp.float32,
                )
            )
        polar = (-2.0 * greens[0] * greens[1]).astype(jnp.bfloat16)
        for m in range(batch):
            for g in range(part // block):
                start = m * part * times + g * span
                total = jnp.dot(
                    mix[...], polar[start : start + span], preferred_element_type=jnp.float32
                )
                spectral[first + m, :, pl.ds(g * block, block), :] = total.astype(
                    jnp.bfloat16
                ).reshape(freqs, block, total.shape[1])
        n = first + batch - 1
        if len(outs) <= 8 or n == places - 1:
            done = slice(first, n + 1) if len(outs) <= 8 else slice(0, places)
            leaving = leaving if first else []
            for r, ref in enumerate(outs):
                to_tm, to_col = tm ^ (r // col_count), p ^ (r % col_count)
                start = to_tm * local_freqs + (to_col // splits) * own_freqs
                pairs = [
                    (spectral.at[m, pl.ds(start, own_freqs)], ref.at[:, m])
                    for m in range(places)[done]
                ]
                leaving += copies_of(pairs, out_sem)
        else:
            leaving = []
    wait_for(leaving)


def pack_kernel(dims, occ, empty, columns, own, other, sem):
    (part, half, tm_count) = dims
    tm = lax.axis_index("tm")
    wide = columns.shape[1]
    pairs = []
    for arr, ref in enumerate((occ, empty)):
        for kt in range(tm_count):
            source = ref.at[pl.ds(pl.multiple_of((tm ^ kt) * part, part), part), :]
            lanes = pl.ds(arr * half, half)
            pairs.append((source, other.at[kt - 1, :, lanes] if kt else own.at[:, lanes]))
    for t in range(tm_count):
        lanes = pl.ds(2 * half + t * wide, wide)
        pairs.append((columns.at[pl.ds(t * part, part), :], own.at[:, lanes]))
    wait_for(copies_of(pairs, sem))


def pick_kernel(lanes, *refs):
    pieces, out, sem = refs[:-2], refs[-2], refs[-1]
    run_copies(
        [(ref.at[:, pl.ds(lanes, out.shape[2])], out.at[n]) for n, ref in enumerate(pieces)], sem
    )


def columns_kernel(keys, dims, *refs):
    (tm_count, row_count, col_count, shard_rows, part) = dims
    pieces = refs[: len(keys)]
    out, own, gathered, own_rows, sem = refs[len(keys) :]
    p = lax.axis_index("col")
    width = row_count * part
    copies = []
    wide = own.shape[0]
    for kc, ref in zip(keys, pieces):
        for kq in range(row_count):
            for t in range(tm_count):
                source = ref.at[kq, :, pl.ds(t * wide, wide)]
                to = pl.multiple_of((t * col_count + (p ^ kc)) * width + kq * part, part)
                copies.append((source, gathered.at[pl.ds(to, part), :]))
                if kq == 0:
                    to = pl.multiple_of((p ^ kc) * shard_rows + t * part, part)
                    copies.append((source, own_rows.at[pl.ds(to, part), :]))
    run_copies(copies, sem)
    out[...] = gathered[...].astype(jnp.float32).T.astype(jnp.bfloat16)
    own[...] = own_rows[...].astype(jnp.float32).T.astype(jnp.bfloat16)


def source_of(r, col_count):
    tm, p = lax.axis_index("tm"), lax.axis_index("col")
    return (tm ^ (r // col_count)) * col_count + (p ^ (r % col_count))


def first_kernel(col_count, all_columns, own, *refs):
    columns_v, own_v, tiles_v, middle_v, sems = refs[-5:]
    (freqs, sources, places, part, rows) = tiles_v.shape
    tiles, outs = refs[:sources], refs[sources : sources + freqs]
    arriving = [copies_of([(all_columns, columns_v), (own, own_v)], sems.at[freqs])]
    arriving += [
        copies_of(
            [
                (ref.at[k], tiles_v.at[k, source_of(r, col_count)])
                for r, ref in enumerate(tiles)
            ],
            sems.at[k],
        )
        for k in range(freqs)
    ]
    wait_for(arriving[0])
    leaving = []
    for k in range(freqs):
        wait_for(arriving[1 + k])
        weights = tiles_v[k].reshape(sources * places * part, rows)
        first = jnp.dot(columns_v[...], weights, preferred_element_type=jnp.float32)
        middle_v[k] = (own_v[...].astype(jnp.float32) + damping * first).astype(jnp.bfloat16)
        leaving += copies_of([(middle_v.at[k], outs[k])], sems.at[freqs + 1])
    wait_for(leaving)


def weights_of(tiles_v, k, index, dims):
    (tm_count, col_count) = dims
    return jnp.concatenate(
        [tiles_v[t * col_count + p, k, index] for p in range(col_count) for t in range(tm_count)],
        axis=0,
    )


def near_kernel(dims, *refs):
    (tm_count, col_count, places) = dims
    sources, count = tm_count * col_count, len(places)
    (out, tiles_v, middles_v, total_v, sems) = refs[-5:]
    tiles, middles = refs[:sources], refs[sources:-5]
    freqs = total_v.shape[0]
    arriving = copies_of(
        [
            (ref.at[:, place], tiles_v.at[source_of(r, col_count), :, n])
            for n, place in enumerate(places)
            for r, ref in enumerate(tiles)
        ],
        sems.at[0],
    )
    arriving += copies_of(
        [(ref, middles_v.at[i // freqs, i % freqs]) for i, ref in enumerate(middles)], sems.at[0]
    )
    wait_for(arriving)
    for k in range(freqs):
        total = None
        for n in range(count):
            weights = weights_of(tiles_v, k, n, dims[:2])
            term = jnp.dot(middles_v[n, k], weights, preferred_element_type=jnp.float32)
            total = term if total is None else total + term
        total_v[k] = total
    wait_for(copies_of([(total_v, out)], sems.at[1]))


def far_kernel(dims, *refs):
    (tm_count, col_count, place, top, shard_rows, other) = dims
    sources = tm_count * col_count
    tiles, total, rest = refs[:sources], refs[sources], refs[sources + 1 :]
    middles, outs = rest[: -5 - top], rest[-5 - top : -5]
    (tiles_v, total_v, middle_v, second_v, sems) = rest[-5:]
    p = lax.axis_index("col")
    freqs = total_v.shape[0]
    span = top * shard_rows
    part_of = p // top
    lane = pl.multiple_of((1 - part_of if other else part_of) * span, span)
    pairs = [
        (ref.at[:, place, :, pl.ds(lane, span)], tiles_v.at[source_of(r, col_count), :, 0])
        for r, ref in enumerate(tiles)
    ]
    pairs += [(total.at[:, :, pl.ds(lane, span)], total_v)]
    pairs += [(ref, middle_v.at[k]) for k, ref in enumerate(middles)]
    wait_for(copies_of(pairs, sems.at[0]))
    for k in range(freqs):
        weights = weights_of(tiles_v, k, 0, dims[:2])
        term = jnp.dot(middle_v[k], weights, preferred_element_type=jnp.float32)
        second = (total_v[k] + term).T.astype(jnp.bfloat16)
        for i in range(top):
            second_v[i, k] = second[i * shard_rows : (i + 1) * shard_rows]
    slot = lax.rem(p, top)
    wait_for(copies_of([(second_v.at[slot ^ d], ref) for d, ref in enumerate(outs)], sems.at[1]))


def final_kernel(keys, splits, columns, *refs):
    pieces, (out, held, columns_v, out_v, sems) = refs[: len(keys)], refs[len(keys) :]
    p = lax.axis_index("col")
    pairs = [(ref, held.at[p ^ k]) for k, ref in zip(keys, pieces)] + [(columns, columns_v)]
    wait_for(copies_of(pairs, sems.at[0]))
    (count, freqs, shard_rows, wide) = held.shape
    step = max(16, shard_rows // 2)
    leaving = []
    for start in range(0, shard_rows, step):
        rows = slice(start, start + step)
        base = columns_v[rows].astype(jnp.float32)
        for source in range(count):
            lane = (source % splits) * wide
            for k in range(freqs):
                value = base[:, lane : lane + wide] + damping * held[source, k, rows].astype(
                    jnp.float32
                )
                out_v[rows, (source // splits) * freqs + k, lane : lane + wide] = value
        leaving += copies_of([(out_v.at[rows], out.at[rows])], sems.at[1])
    wait_for(leaving)


def shards(occ_orbitals, empty_orbitals, occ_rate, empty_rate, columns):
    tm_count, row_count, col_count = (lax.axis_size(a) for a in ("tm", "row", "col"))
    shard_rows, half = occ_orbitals.shape
    columns_wide = columns.shape[1]
    orbitals = tm_count * half
    part = shard_rows // tm_count
    width = row_count * part
    tile_rows = col_count * shard_rows
    col_index = lax.axis_index("col")
    both = (occ_orbitals, empty_orbitals)
    sources = tm_count * col_count
    local_freqs = NF // tm_count
    own_freqs = max(1, local_freqs // col_count)
    splits = max(1, col_count // local_freqs)
    columns_own = columns_wide // splits
    high, low = bits_of(col_count)[:-1], bits_of(col_count)[-1:]

    rows_of = [{(arr, 0, 0): value} for arr, value in enumerate(both)]
    own, other = pl.pallas_call(
        functools.partial(pack_kernel, (part, half, tm_count)),
        out_shape=(
            jax.ShapeDtypeStruct((part, 2 * half + tm_count * columns_wide), jnp.bfloat16),
            jax.ShapeDtypeStruct((tm_count - 1, part, 2 * half), jnp.bfloat16),
        ),
        in_specs=[HBM] * 3,
        out_specs=(VMEM, VMEM),
        scratch_shapes=[pltpu.SemaphoreType.DMA],
        compiler_params=FULL,
        name="pack",
    )(occ_orbitals, empty_orbitals, columns)
    got = [
        swap(other[kt - 1], "tm", kt) if tm_count > 2 else swap(other.reshape(part, -1), "tm", kt)
        for kt in range(1, tm_count)
    ]
    for bit in bits_of(tm_count):
        rows_of = [spread(pieces, "tm", bit, 1) for pieces in rows_of]
    near = [{k: v for k, v in pieces.items() if k[1] == 0} for pieces in rows_of]
    far = [{k: v for k, v in pieces.items() if k[1] != 0} for pieces in rows_of]
    for bit in high:
        near = [spread(pieces, "col", bit, 2) for pieces in near]
    streams, late = (0,), tuple(range(1, tm_count))
    cols_of = {(0, streams): own, (0, late): jnp.concatenate(got, axis=1) if len(got) > 1 else got[0]}

    def ring_step(group, source, target, step):
        cols_of[(target, group)] = shift(cols_of[(source, group)], "row", step)

    behind = (row_count - 1) // 2
    ahead = row_count // 2
    ring_step(streams, 0, 1, -1)
    if behind:
        ring_step(streams, 0, row_count - 1, 1)
    for bit in high:
        far = [spread(pieces, "col", bit, 2) for pieces in far]
    if behind:
        ring_step(late, 0, row_count - 1, 1)
    ring_step(late, 0, 1, -1)
    for k in range(2, ahead + 1):
        ring_step(streams, k - 1, k, -1)
    for k in range(2, behind + 1):
        ring_step(streams, row_count - k + 1, row_count - k, 1)
    for bit in low:
        near = [spread(pieces, "col", bit, 2) for pieces in near]
    for k in range(2, ahead + 1):
        ring_step(late, k - 1, k, -1)
    for k in range(2, behind + 1):
        ring_step(late, row_count - k + 1, row_count - k, 1)
    for bit in low:
        far = [spread(pieces, "col", bit, 2) for pieces in far]
    row_pieces = {**near[0], **near[1], **far[0], **far[1]}
    row_keys = list(row_pieces)

    picked = pl.pallas_call(
        functools.partial(pick_kernel, 2 * half),
        out_shape=jax.ShapeDtypeStruct((row_count, part, tm_count * columns_wide), jnp.bfloat16),
        in_specs=[HBM] * row_count,
        out_specs=VMEM,
        scratch_shapes=[pltpu.SemaphoreType.DMA],
        compiler_params=FULL,
        name="pick",
    )(*[cols_of[(kq, streams)] for kq in range(row_count)])
    column_pieces = {(0,): picked}
    for bit in high:
        column_pieces = spread(column_pieces, "col", bit, 0)
    for bit in low:
        column_pieces = spread(column_pieces, "col", bit, 0)

    cosine = time_tables(NT, NF)[1]
    rates = [rate.reshape(1, -1) for rate in (occ_rate, empty_rate)]
    block = min(16, part)
    mix = jnp.asarray(np.kron(cosine.astype(np.float32), np.eye(block)).astype(jnp.bfloat16))
    groups = [streams, late]
    pieces = [cols_of[(place, kts)] for place in range(row_count) for kts in groups]
    sent = pl.pallas_call(
        functools.partial(
            tile_kernel,
            row_keys,
            groups,
            (NT, NF, half, shard_rows, row_count, col_count, own_freqs, splits),
        ),
        out_shape=[
            jax.ShapeDtypeStruct((own_freqs, row_count, part, tile_rows), jnp.bfloat16)
        ]
        * sources,
        in_specs=[VMEM] * 3 + [HBM] * (len(row_keys) + len(pieces)),
        out_specs=[HBM] * sources,
        scratch_shapes=[
            pltpu.VMEM((2, tile_rows, orbitals), jnp.bfloat16),
            pltpu.VMEM((2, row_count, part, orbitals), jnp.bfloat16),
            pltpu.VMEM((2, BATCH * NT * part, orbitals), jnp.bfloat16),
            pltpu.VMEM((2, NT, orbitals), jnp.float32),
            pltpu.VMEM((row_count, NF, part, tile_rows), jnp.bfloat16),
            pltpu.SemaphoreType.DMA((2,)),
            pltpu.SemaphoreType.DMA,
        ],
        compiler_params=FULL,
        name="tile",
    )(mix, *rates, *[row_pieces[k] for k in row_keys], *pieces)

    keys = [key[0] for key in column_pieces]
    all_columns, own_columns = pl.pallas_call(
        functools.partial(columns_kernel, keys, (tm_count, row_count, col_count, shard_rows, part)),
        out_shape=(
            jax.ShapeDtypeStruct((columns_wide, tm_count * col_count * width), jnp.bfloat16),
            jax.ShapeDtypeStruct((columns_wide, tile_rows), jnp.bfloat16),
        ),
        in_specs=[HBM] * len(keys),
        out_specs=(VMEM, VMEM),
        scratch_shapes=[
            pltpu.VMEM((tm_count * col_count * width, columns_wide), jnp.bfloat16),
            pltpu.VMEM((tile_rows, columns_wide), jnp.bfloat16),
            pltpu.SemaphoreType.DMA,
        ],
        compiler_params=FULL,
        name="columns",
    )(*column_pieces.values())

    if splits > 1:
        first_row = (col_index % splits) * columns_own
        all_columns = lax.dynamic_slice_in_dim(all_columns, first_row, columns_own, 0)
        own_columns = lax.dynamic_slice_in_dim(own_columns, first_row, columns_own, 0)
    far_first = sorted(range(1, sources), key=lambda r: -(r >= col_count) - (r % col_count > 1))
    tiles = [sent[0]] * sources
    for r in far_first:
        pairs = [(i, i ^ r) for i in range(sources)]
        tiles[r] = lax.ppermute(sent[r], ("tm", "col"), pairs)

    first_shape = (own_freqs, columns_own, tile_rows)
    middle = pl.pallas_call(
        functools.partial(first_kernel, col_count),
        out_shape=[jax.ShapeDtypeStruct(first_shape[1:], jnp.bfloat16)] * own_freqs,
        in_specs=[HBM] * (2 + sources),
        out_specs=[HBM] * own_freqs,
        scratch_shapes=[
            pltpu.VMEM((columns_own, sources * width), jnp.bfloat16),
            pltpu.VMEM((columns_own, tile_rows), jnp.bfloat16),
            pltpu.VMEM((own_freqs, sources, row_count, part, tile_rows), jnp.bfloat16),
            pltpu.VMEM(first_shape, jnp.bfloat16),
            pltpu.SemaphoreType.DMA((own_freqs + 2,)),
        ],
        compiler_params=FULL,
        name="first",
    )(all_columns, own_columns, *tiles)
    middles = {(0, k): value for k, value in enumerate(middle)}

    def middle_step(source, target, step):
        for k in range(own_freqs):
            middles[(target, k)] = shift(middles[(source, k)], "row", step)

    middle_step(0, 1, -1)
    for k in range(1, behind + 1):
        middle_step((row_count - k + 1) % row_count, row_count - k, 1)
    for k in range(2, ahead + 1):
        middle_step(k - 1, k, -1)
    own_range = range(own_freqs)
    last = ahead
    places = [k for k in range(row_count) if k != last]
    total = pl.pallas_call(
        functools.partial(near_kernel, (tm_count, col_count, places)),
        out_shape=jax.ShapeDtypeStruct(first_shape, jnp.float32),
        in_specs=[HBM] * (sources + len(places) * own_freqs),
        out_specs=HBM,
        scratch_shapes=[
            pltpu.VMEM((sources, own_freqs, len(places), part, tile_rows), jnp.bfloat16),
            pltpu.VMEM((len(places),) + first_shape, jnp.bfloat16),
            pltpu.VMEM(first_shape, jnp.float32),
            pltpu.SemaphoreType.DMA((2,)),
        ],
        compiler_params=FULL,
        name="near",
    )(*tiles, *[middles[(place, k)] for place in places for k in own_range])
    top = col_count // 2
    span = top * shard_rows
    seconds = []
    for other in (True, False):
        seconds.append(
            pl.pallas_call(
                functools.partial(far_kernel, (tm_count, col_count, last, top, shard_rows, other)),
                out_shape=[jax.ShapeDtypeStruct((own_freqs, shard_rows, columns_own), jnp.bfloat16)]
                * top,
                in_specs=[HBM] * (sources + 1 + own_freqs),
                out_specs=[HBM] * top,
                scratch_shapes=[
                    pltpu.VMEM((sources, own_freqs, 1, part, span), jnp.bfloat16),
                    pltpu.VMEM((own_freqs, columns_own, span), jnp.float32),
                    pltpu.VMEM(first_shape, jnp.bfloat16),
                    pltpu.VMEM((top, own_freqs, shard_rows, columns_own), jnp.bfloat16),
                    pltpu.SemaphoreType.DMA((2,)),
                ],
                compiler_params=FULL,
            )(*tiles, total, *[middles[(last, k)] for k in own_range])
        )
    parts = {0: seconds[1][0]}
    for group, start in ((seconds[0], top), (seconds[1], 0)):
        for d, value in enumerate(group):
            if start + d:
                parts[start + d] = swap(value, "col", start + d)
    return pl.pallas_call(
        functools.partial(final_kernel, list(parts), splits),
        out_shape=jax.ShapeDtypeStruct((shard_rows, local_freqs, columns_wide), jnp.float32),
        in_specs=[HBM] * (1 + len(parts)),
        out_specs=HBM,
        scratch_shapes=[
            pltpu.VMEM((col_count, own_freqs, shard_rows, columns_own), jnp.bfloat16),
            pltpu.VMEM((shard_rows, columns_wide), jnp.bfloat16),
            pltpu.VMEM((shard_rows, local_freqs, columns_wide), jnp.float32),
            pltpu.SemaphoreType.DMA((2,)),
        ],
        compiler_params=FULL,
        name="final",
    )(columns, *parts.values())


def solution(mesh):
    placed = (P(("col", "row"), "tm"), P(("col", "row"), "tm"), P(), P(), P(("col", "row"), None))
    return jax.shard_map(
        shards, mesh=mesh, in_specs=placed, out_specs=P(("col", "row"), "tm", None), check_vma=False
    )
```

```python
import functools

import jax
import jax.numpy as jnp
import numpy as np
from jax import lax
from jax.experimental import pallas as pl
from jax.experimental.pallas import tpu as pltpu
from jax.sharding import PartitionSpec as P

NT = 16
NF = 16

damping = 0.3

BATCH = 1

FULL = pltpu.CompilerParams(vmem_limit_bytes=67043328)
HBM = pl.BlockSpec(memory_space=pltpu.HBM)
VMEM = pl.BlockSpec(memory_space=pltpu.VMEM)
SMEM = pl.BlockSpec(memory_space=pltpu.SMEM)


def time_tables(count_times, count_freqs):
    moments = np.float32(0.25) * (np.arange(count_times, dtype=np.float32) + np.float32(0.5))
    omegas = np.float32(0.4) * (np.arange(count_freqs, dtype=np.float32) + np.float32(0.5))
    cosine = np.float32(0.5) * np.cos(omegas[:, None] * moments[None, :])
    return (moments, cosine.astype(jnp.bfloat16))


def swap(value, axis, bit):
    size = lax.axis_size(axis)
    return lax.ppermute(value, axis, [(i, i ^ bit) for i in range(size)])


def shift(value, axis, step):
    size = lax.axis_size(axis)
    return lax.ppermute(value, axis, [(i, (i + step) % size) for i in range(size)])


def bits_of(count):
    return [1 << b for b in reversed(range(count.bit_length() - 1))]


def spread(pieces, axis, bit, slot):
    out = dict(pieces)
    for key, value in pieces.items():
        moved = list(key)
        moved[slot] ^= bit
        out[tuple(moved)] = swap(value, axis, bit)
    return out


def run_copies(copies, sem):
    copies = [pltpu.make_async_copy(a, b, sem) for a, b in copies]
    for copy in copies:
        copy.start()
    for copy in copies:
        copy.wait()


def copies_of(pairs, sem):
    copies = [pltpu.make_async_copy(a, b, sem) for a, b in pairs]
    for copy in copies:
        copy.start()
    return copies


def wait_for(copies):
    for copy in copies:
        copy.wait()


def tile_kernel(row_keys, groups, dims, mix, occ_rate, empty_rate, *refs):
    (times, freqs, half, shard_rows, places, col_count, own_freqs, splits) = dims
    row_pieces = refs[: len(row_keys)]
    pieces = refs[len(row_pieces) :][: places * len(groups)]
    rest = refs[len(row_pieces) + len(pieces) :]
    outs, (rows, cols, scaled, factors, spectral, sems, out_sem) = rest[:-7], rest[-7:]
    tm, p = lax.axis_index("tm"), lax.axis_index("col")
    part = cols.shape[2]
    local_freqs = freqs // (len(outs) // col_count)
    pairs = [[], []]
    for n in range(places):
        for i, kts in enumerate(groups):
            ref = pieces[n * len(groups) + i]
            for m, (kt, arr) in enumerate((kt, arr) for kt in kts for arr in range(2)):
                lane = pl.multiple_of((tm ^ kt) * half, half)
                to = cols.at[arr, n, :, pl.ds(lane, half)]
                pairs[arr].append((ref.at[:, pl.ds(m * half, half)], to))
    for (arr, kt, kc), ref in zip(row_keys, row_pieces):
        to = pl.multiple_of((p ^ kc) * shard_rows, shard_rows)
        lane = pl.multiple_of((tm ^ kt) * half, half)
        pairs[arr].append((ref, rows.at[arr, pl.ds(to, shard_rows), pl.ds(lane, half)]))
    arriving = [copies_of(pairs[arr], sems.at[arr]) for arr in range(2)]
    steps = lax.broadcasted_iota(jnp.int32, factors.shape[1:], 0).astype(jnp.float32)
    for arr, rate in enumerate((occ_rate, empty_rate)):
        factors[arr] = jnp.exp(-rate[...] * (0.25 * (steps + 0.5)))
    block = mix.shape[0] // freqs
    span = block * times
    batch = scaled.shape[1] // (part * times)
    for first in range(0, places, batch):
        greens = []
        for arr in range(2):
            if first == 0:
                wait_for(arriving[arr])
            for m in range(batch):
                for g in range(part // block):
                    values = cols[arr, first + m, pl.ds(g * block, block), :].astype(jnp.float32)
                    start = m * part * times + g * span
                    for j in range(times):
                        factor = factors[arr, pl.ds(j, 1), :]
                        scaled[arr, pl.ds(start + j * block, block), :] = (values * factor).astype(
                            jnp.bfloat16
                        )
            greens.append(
                lax.dot_general(
                    scaled[arr],
                    rows[arr],
                    (((1,), (1,)), ((), ())),
                    preferred_element_type=jnp.float32,
                )
            )
        polar = (-2.0 * greens[0] * greens[1]).astype(jnp.bfloat16)
        for m in range(batch):
            for g in range(part // block):
                start = m * part * times + g * span
                total = jnp.dot(
                    mix[...], polar[start : start + span], preferred_element_type=jnp.float32
                )
                spectral[first + m, :, pl.ds(g * block, block), :] = total.astype(
                    jnp.bfloat16
                ).reshape(freqs, block, total.shape[1])
        n = first + batch - 1
        if len(outs) <= 8 or n == places - 1:
            done = slice(first, n + 1) if len(outs) <= 8 else slice(0, places)
            leaving = leaving if first else []
            for r, ref in enumerate(outs):
                to_tm, to_col = tm ^ (r // col_count), p ^ (r % col_count)
                start = to_tm * local_freqs + (to_col // splits) * own_freqs
                pairs = [
                    (spectral.at[m, pl.ds(start, own_freqs)], ref.at[:, m])
                    for m in range(places)[done]
                ]
                leaving += copies_of(pairs, out_sem)
        else:
            leaving = []
    wait_for(leaving)


def pack_kernel(dims, occ, empty, columns, own, other, sem):
    (part, half, tm_count) = dims
    tm = lax.axis_index("tm")
    wide = columns.shape[1]
    pairs = []
    for arr, ref in enumerate((occ, empty)):
        for kt in range(tm_count):
            source = ref.at[pl.ds(pl.multiple_of((tm ^ kt) * part, part), part), :]
            lanes = pl.ds(arr * half, half)
            pairs.append((source, other.at[kt - 1, :, lanes] if kt else own.at[:, lanes]))
    for t in range(tm_count):
        lanes = pl.ds(2 * half + t * wide, wide)
        pairs.append((columns.at[pl.ds(t * part, part), :], own.at[:, lanes]))
    wait_for(copies_of(pairs, sem))


def pick_kernel(lanes, *refs):
    pieces, out, sem = refs[:-2], refs[-2], refs[-1]
    run_copies(
        [(ref.at[:, pl.ds(lanes, out.shape[2])], out.at[n]) for n, ref in enumerate(pieces)], sem
    )


def columns_kernel(keys, dims, *refs):
    (tm_count, row_count, col_count, shard_rows, part) = dims
    pieces = refs[: len(keys)]
    out, own, gathered, own_rows, sem = refs[len(keys) :]
    p = lax.axis_index("col")
    width = row_count * part
    copies = []
    wide = own.shape[0]
    for kc, ref in zip(keys, pieces):
        for kq in range(row_count):
            for t in range(tm_count):
                source = ref.at[kq, :, pl.ds(t * wide, wide)]
                to = pl.multiple_of((t * col_count + (p ^ kc)) * width + kq * part, part)
                copies.append((source, gathered.at[pl.ds(to, part), :]))
                if kq == 0:
                    to = pl.multiple_of((p ^ kc) * shard_rows + t * part, part)
                    copies.append((source, own_rows.at[pl.ds(to, part), :]))
    run_copies(copies, sem)
    out[...] = gathered[...].astype(jnp.float32).T.astype(jnp.bfloat16)
    own[...] = own_rows[...].astype(jnp.float32).T.astype(jnp.bfloat16)


def source_of(r, col_count):
    tm, p = lax.axis_index("tm"), lax.axis_index("col")
    return (tm ^ (r // col_count)) * col_count + (p ^ (r % col_count))


def first_kernel(dims, all_columns, own, *refs):
    (col_count, k) = dims
    out, columns_v, own_v, tiles_v, middle_v, sem = refs[-6:]
    tiles = refs[:-6]
    (sources, places, part, rows) = tiles_v.shape
    pairs = [(ref.at[k], tiles_v.at[source_of(r, col_count)]) for r, ref in enumerate(tiles)]
    wait_for(copies_of(pairs + [(all_columns, columns_v), (own, own_v)], sem))
    weights = tiles_v[...].reshape(sources * places * part, rows)
    first = jnp.dot(columns_v[...], weights, preferred_element_type=jnp.float32)
    middle_v[...] = (own_v[...].astype(jnp.float32) + damping * first).astype(jnp.bfloat16)
    wait_for(copies_of([(middle_v, out)], sem))


def weights_of(tiles_v, k, index, dims):
    (tm_count, col_count) = dims
    return jnp.concatenate(
        [tiles_v[t * col_count + p, k, index] for p in range(col_count) for t in range(tm_count)],
        axis=0,
    )


def near_kernel(dims, *refs):
    (tm_count, col_count, places) = dims
    sources, count = tm_count * col_count, len(places)
    (out, tiles_v, middles_v, total_v, sems) = refs[-5:]
    tiles, middles = refs[:sources], refs[sources:-5]
    freqs = total_v.shape[0]
    arriving = copies_of(
        [
            (ref.at[:, place], tiles_v.at[source_of(r, col_count), :, n])
            for n, place in enumerate(places)
            for r, ref in enumerate(tiles)
        ],
        sems.at[0],
    )
    arriving += copies_of(
        [(ref, middles_v.at[i // freqs, i % freqs]) for i, ref in enumerate(middles)], sems.at[0]
    )
    wait_for(arriving)
    for k in range(freqs):
        total = None
        for n in range(count):
            weights = weights_of(tiles_v, k, n, dims[:2])
            term = jnp.dot(middles_v[n, k], weights, preferred_element_type=jnp.float32)
            total = term if total is None else total + term
        total_v[k] = total
    wait_for(copies_of([(total_v, out)], sems.at[1]))


def far_kernel(dims, *refs):
    (tm_count, col_count, place, top, shard_rows, other) = dims
    sources = tm_count * col_count
    tiles, total, rest = refs[:sources], refs[sources], refs[sources + 1 :]
    middles, outs = rest[: -5 - top], rest[-5 - top : -5]
    (tiles_v, total_v, middle_v, second_v, sems) = rest[-5:]
    p = lax.axis_index("col")
    freqs = total_v.shape[0]
    span = top * shard_rows
    part_of = p // top
    lane = pl.multiple_of((1 - part_of if other else part_of) * span, span)
    pairs = [
        (ref.at[:, place, :, pl.ds(lane, span)], tiles_v.at[source_of(r, col_count), :, 0])
        for r, ref in enumerate(tiles)
    ]
    pairs += [(total.at[:, :, pl.ds(lane, span)], total_v)]
    pairs += [(ref, middle_v.at[k]) for k, ref in enumerate(middles)]
    wait_for(copies_of(pairs, sems.at[0]))
    for k in range(freqs):
        weights = weights_of(tiles_v, k, 0, dims[:2])
        term = jnp.dot(middle_v[k], weights, preferred_element_type=jnp.float32)
        second = (total_v[k] + term).T.astype(jnp.bfloat16)
        for i in range(top):
            second_v[i, k] = second[i * shard_rows : (i + 1) * shard_rows]
    slot = lax.rem(p, top)
    wait_for(copies_of([(second_v.at[slot ^ d], ref) for d, ref in enumerate(outs)], sems.at[1]))


def final_kernel(keys, splits, columns, *refs):
    pieces, (out, held, columns_v, out_v, sems) = refs[: len(keys)], refs[len(keys) :]
    p = lax.axis_index("col")
    pairs = [(ref, held.at[p ^ k]) for k, ref in zip(keys, pieces)] + [(columns, columns_v)]
    wait_for(copies_of(pairs, sems.at[0]))
    (count, freqs, shard_rows, wide) = held.shape
    step = max(16, shard_rows // 2)
    leaving = []
    for start in range(0, shard_rows, step):
        rows = slice(start, start + step)
        base = columns_v[rows].astype(jnp.float32)
        for source in range(count):
            lane = (source % splits) * wide
            for k in range(freqs):
                value = base[:, lane : lane + wide] + damping * held[source, k, rows].astype(
                    jnp.float32
                )
                out_v[rows, (source // splits) * freqs + k, lane : lane + wide] = value
        leaving += copies_of([(out_v.at[rows], out.at[rows])], sems.at[1])
    wait_for(leaving)


def shards(occ_orbitals, empty_orbitals, occ_rate, empty_rate, columns):
    tm_count, row_count, col_count = (lax.axis_size(a) for a in ("tm", "row", "col"))
    shard_rows, half = occ_orbitals.shape
    columns_wide = columns.shape[1]
    orbitals = tm_count * half
    part = shard_rows // tm_count
    width = row_count * part
    tile_rows = col_count * shard_rows
    col_index = lax.axis_index("col")
    both = (occ_orbitals, empty_orbitals)
    sources = tm_count * col_count
    local_freqs = NF // tm_count
    own_freqs = max(1, local_freqs // col_count)
    splits = max(1, col_count // local_freqs)
    columns_own = columns_wide // splits
    high, low = bits_of(col_count)[:-1], bits_of(col_count)[-1:]

    rows_of = [{(arr, 0, 0): value} for arr, value in enumerate(both)]
    own, other = pl.pallas_call(
        functools.partial(pack_kernel, (part, half, tm_count)),
        out_shape=(
            jax.ShapeDtypeStruct((part, 2 * half + tm_count * columns_wide), jnp.bfloat16),
            jax.ShapeDtypeStruct((tm_count - 1, part, 2 * half), jnp.bfloat16),
        ),
        in_specs=[HBM] * 3,
        out_specs=(VMEM, VMEM),
        scratch_shapes=[pltpu.SemaphoreType.DMA],
        compiler_params=FULL,
        name="pack",
    )(occ_orbitals, empty_orbitals, columns)
    got = [
        swap(other[kt - 1], "tm", kt) if tm_count > 2 else swap(other.reshape(part, -1), "tm", kt)
        for kt in range(1, tm_count)
    ]
    for bit in bits_of(tm_count):
        rows_of = [spread(pieces, "tm", bit, 1) for pieces in rows_of]
    near = [{k: v for k, v in pieces.items() if k[1] == 0} for pieces in rows_of]
    far = [{k: v for k, v in pieces.items() if k[1] != 0} for pieces in rows_of]
    for bit in high:
        near = [spread(pieces, "col", bit, 2) for pieces in near]
    streams, late = (0,), tuple(range(1, tm_count))
    cols_of = {(0, streams): own, (0, late): jnp.concatenate(got, axis=1) if len(got) > 1 else got[0]}

    def ring_step(group, source, target, step):
        cols_of[(target, group)] = shift(cols_of[(source, group)], "row", step)

    behind = (row_count - 1) // 2
    ahead = row_count // 2
    ring_step(streams, 0, 1, -1)
    if behind:
        ring_step(streams, 0, row_count - 1, 1)
    for bit in high:
        far = [spread(pieces, "col", bit, 2) for pieces in far]
    if behind:
        ring_step(late, 0, row_count - 1, 1)
    ring_step(late, 0, 1, -1)
    for k in range(2, ahead + 1):
        ring_step(streams, k - 1, k, -1)
    for k in range(2, behind + 1):
        ring_step(streams, row_count - k + 1, row_count - k, 1)
    for bit in low:
        near = [spread(pieces, "col", bit, 2) for pieces in near]
    for k in range(2, ahead + 1):
        ring_step(late, k - 1, k, -1)
    for k in range(2, behind + 1):
        ring_step(late, row_count - k + 1, row_count - k, 1)
    for bit in low:
        far = [spread(pieces, "col", bit, 2) for pieces in far]
    row_pieces = {**near[0], **near[1], **far[0], **far[1]}
    row_keys = list(row_pieces)

    picked = pl.pallas_call(
        functools.partial(pick_kernel, 2 * half),
        out_shape=jax.ShapeDtypeStruct((row_count, part, tm_count * columns_wide), jnp.bfloat16),
        in_specs=[HBM] * row_count,
        out_specs=VMEM,
        scratch_shapes=[pltpu.SemaphoreType.DMA],
        compiler_params=FULL,
        name="pick",
    )(*[cols_of[(kq, streams)] for kq in range(row_count)])
    column_pieces = {(0,): picked}
    for bit in high:
        column_pieces = spread(column_pieces, "col", bit, 0)
    for bit in low:
        column_pieces = spread(column_pieces, "col", bit, 0)

    cosine = time_tables(NT, NF)[1]
    rates = [rate.reshape(1, -1) for rate in (occ_rate, empty_rate)]
    block = min(16, part)
    mix = jnp.asarray(np.kron(cosine.astype(np.float32), np.eye(block)).astype(jnp.bfloat16))
    groups = [streams, late]
    pieces = [cols_of[(place, kts)] for place in range(row_count) for kts in groups]
    sent = pl.pallas_call(
        functools.partial(
            tile_kernel,
            row_keys,
            groups,
            (NT, NF, half, shard_rows, row_count, col_count, own_freqs, splits),
        ),
        out_shape=[
            jax.ShapeDtypeStruct((own_freqs, row_count, part, tile_rows), jnp.bfloat16)
        ]
        * sources,
        in_specs=[VMEM] * 3 + [HBM] * (len(row_keys) + len(pieces)),
        out_specs=[HBM] * sources,
        scratch_shapes=[
            pltpu.VMEM((2, tile_rows, orbitals), jnp.bfloat16),
            pltpu.VMEM((2, row_count, part, orbitals), jnp.bfloat16),
            pltpu.VMEM((2, BATCH * NT * part, orbitals), jnp.bfloat16),
            pltpu.VMEM((2, NT, orbitals), jnp.float32),
            pltpu.VMEM((row_count, NF, part, tile_rows), jnp.bfloat16),
            pltpu.SemaphoreType.DMA((2,)),
            pltpu.SemaphoreType.DMA,
        ],
        compiler_params=FULL,
        name="tile",
    )(mix, *rates, *[row_pieces[k] for k in row_keys], *pieces)

    keys = [key[0] for key in column_pieces]
    all_columns, own_columns = pl.pallas_call(
        functools.partial(columns_kernel, keys, (tm_count, row_count, col_count, shard_rows, part)),
        out_shape=(
            jax.ShapeDtypeStruct((columns_wide, tm_count * col_count * width), jnp.bfloat16),
            jax.ShapeDtypeStruct((columns_wide, tile_rows), jnp.bfloat16),
        ),
        in_specs=[HBM] * len(keys),
        out_specs=(VMEM, VMEM),
        scratch_shapes=[
            pltpu.VMEM((tm_count * col_count * width, columns_wide), jnp.bfloat16),
            pltpu.VMEM((tile_rows, columns_wide), jnp.bfloat16),
            pltpu.SemaphoreType.DMA,
        ],
        compiler_params=FULL,
        name="columns",
    )(*column_pieces.values())

    if splits > 1:
        first_row = (col_index % splits) * columns_own
        all_columns = lax.dynamic_slice_in_dim(all_columns, first_row, columns_own, 0)
        own_columns = lax.dynamic_slice_in_dim(own_columns, first_row, columns_own, 0)
    far_first = sorted(range(1, sources), key=lambda r: -(r >= col_count) - (r % col_count > 1))
    tiles = [sent[0]] * sources
    for r in far_first:
        pairs = [(i, i ^ r) for i in range(sources)]
        tiles[r] = lax.ppermute(sent[r], ("tm", "col"), pairs)

    first_shape = (own_freqs, columns_own, tile_rows)
    middles = {}
    for k in range(own_freqs):
        middles[(0, k)] = pl.pallas_call(
            functools.partial(first_kernel, (col_count, k)),
            out_shape=jax.ShapeDtypeStruct(first_shape[1:], jnp.bfloat16),
            in_specs=[HBM] * (2 + sources),
            out_specs=HBM,
            scratch_shapes=[
                pltpu.VMEM((columns_own, sources * width), jnp.bfloat16),
                pltpu.VMEM((columns_own, tile_rows), jnp.bfloat16),
                pltpu.VMEM((sources, row_count, part, tile_rows), jnp.bfloat16),
                pltpu.VMEM(first_shape[1:], jnp.bfloat16),
                pltpu.SemaphoreType.DMA,
            ],
            compiler_params=FULL,
        )(all_columns, own_columns, *tiles)

    def middle_step(source, target, step):
        for k in range(own_freqs):
            middles[(target, k)] = shift(middles[(source, k)], "row", step)

    middle_step(0, 1, -1)
    for k in range(1, behind + 1):
        middle_step((row_count - k + 1) % row_count, row_count - k, 1)
    for k in range(2, ahead + 1):
        middle_step(k - 1, k, -1)
    own_range = range(own_freqs)
    last = ahead
    places = [k for k in range(row_count) if k != last]
    total = pl.pallas_call(
        functools.partial(near_kernel, (tm_count, col_count, places)),
        out_shape=jax.ShapeDtypeStruct(first_shape, jnp.float32),
        in_specs=[HBM] * (sources + len(places) * own_freqs),
        out_specs=HBM,
        scratch_shapes=[
            pltpu.VMEM((sources, own_freqs, len(places), part, tile_rows), jnp.bfloat16),
            pltpu.VMEM((len(places),) + first_shape, jnp.bfloat16),
            pltpu.VMEM(first_shape, jnp.float32),
            pltpu.SemaphoreType.DMA((2,)),
        ],
        compiler_params=FULL,
        name="near",
    )(*tiles, *[middles[(place, k)] for place in places for k in own_range])
    top = col_count // 2
    span = top * shard_rows
    seconds = []
    for other in (True, False):
        seconds.append(
            pl.pallas_call(
                functools.partial(far_kernel, (tm_count, col_count, last, top, shard_rows, other)),
                out_shape=[jax.ShapeDtypeStruct((own_freqs, shard_rows, columns_own), jnp.bfloat16)]
                * top,
                in_specs=[HBM] * (sources + 1 + own_freqs),
                out_specs=[HBM] * top,
                scratch_shapes=[
                    pltpu.VMEM((sources, own_freqs, 1, part, span), jnp.bfloat16),
                    pltpu.VMEM((own_freqs, columns_own, span), jnp.float32),
                    pltpu.VMEM(first_shape, jnp.bfloat16),
                    pltpu.VMEM((top, own_freqs, shard_rows, columns_own), jnp.bfloat16),
                    pltpu.SemaphoreType.DMA((2,)),
                ],
                compiler_params=FULL,
            )(*tiles, total, *[middles[(last, k)] for k in own_range])
        )
    parts = {0: seconds[1][0]}
    for group, start in ((seconds[0], top), (seconds[1], 0)):
        for d, value in enumerate(group):
            if start + d:
                parts[start + d] = swap(value, "col", start + d)
    return pl.pallas_call(
        functools.partial(final_kernel, list(parts), splits),
        out_shape=jax.ShapeDtypeStruct((shard_rows, local_freqs, columns_wide), jnp.float32),
        in_specs=[HBM] * (1 + len(parts)),
        out_specs=HBM,
        scratch_shapes=[
            pltpu.VMEM((col_count, own_freqs, shard_rows, columns_own), jnp.bfloat16),
            pltpu.VMEM((shard_rows, columns_wide), jnp.bfloat16),
            pltpu.VMEM((shard_rows, local_freqs, columns_wide), jnp.float32),
            pltpu.SemaphoreType.DMA((2,)),
        ],
        compiler_params=FULL,
        name="final",
    )(columns, *parts.values())


def solution(mesh):
    placed = (P(("col", "row"), "tm"), P(("col", "row"), "tm"), P(), P(), P(("col", "row"), None))
    return jax.shard_map(
        shards, mesh=mesh, in_specs=placed, out_specs=P(("col", "row"), "tm", None), check_vma=False
    )
```
